256 devices in a mesh: pair: 2 (over z_lo), ctx: 16 (over x, y), head: 8 (over z_hi, core).
Axes of the slice: x: 4, y: 4, z: 8 (z_hi: 4, z_lo: 2; z = z_hi * 2 + z_lo), core: 2. Of those that a mesh axis runs over, the one named last changes fastest.
Arguments:
- prompt_queries: bfloat16 [2048, 8192], P(('pair', 'ctx'), 'head'), may hold values from -128 to 128
- prompt_key_rows: bfloat16 [2048, 1024], P(('pair', 'ctx'), 'head'), may hold values from -8 to 8
- prompt_value_rows: bfloat16 [2048, 1024], P(('pair', 'ctx'), 'head'), may hold values from -6 to 6
- answer_queries: bfloat16 [2, 1024, 8192], P('pair', 'ctx', 'head'), may hold values from -128 to 128
- response_key_rows: bfloat16 [2, 1024, 1024], P('pair', 'ctx', 'head'), may hold values from -8 to 8
- response_value_rows: bfloat16 [2, 1024, 1024], P('pair', 'ctx', 'head'), may hold values from -6 to 6
- prompt_cotangent: bfloat16 [2048, 8192], P(('pair', 'ctx'), 'head'), may hold values from -6 to 6
- answer_cotangent: bfloat16 [2, 1024, 8192], P('pair', 'ctx', 'head'), may hold values from -6 to 6
- prompt_length: int32 [1], replicated, may hold values from 1025 to 2048
- answer_lengths: int32 [2], replicated, may hold values from 513 to 1024
Outputs:
- prompt_attended: bfloat16 [2048, 8192], P(('pair', 'ctx'), 'head')
- answer_attended: bfloat16 [2, 1024, 8192], P('pair', 'ctx', 'head')
- prompt_query_grad: bfloat16 [2048, 8192], P(('pair', 'ctx'), 'head')
- prompt_key_gradient: bfloat16 [2048, 1024], P(('pair', 'ctx'), 'head')
- prompt_value_gradient: bfloat16 [2048, 1024], P(('pair', 'ctx'), 'head')
- answer_query_grad: bfloat16 [2, 1024, 8192], P('pair', 'ctx', 'head')
- response_key_gradient: bfloat16 [2, 1024, 1024], P('pair', 'ctx', 'head')
- response_value_gradient: bfloat16 [2, 1024, 1024], P('pair', 'ctx', 'head')
The draws below stay inside these ranges and needn't reach their ends.
All inputs are finite; a program needn't handle non-finite values.
Results may differ from the reference program's by a relative error of at most 0.0054.
Values may be sent and summed in bfloat16 or wider, within the bound.
No kernel may reach another device: no remote copies, remote signals or barrier semaphores. Data moves between devices by JAX's collectives and lax.ppermute only.
A program may use at most 64 MiB of HBM per device.

```python
import jax
import jax.numpy as jnp
from jax import lax

QUERY_HEADS = 64
KEY_VALUE_HEADS = 8
HEAD_SIZE = 128
PROMPT_TOKENS = 2048
RESPONSE_TOKENS = 1024


def joint_draw(key):
    query_group_count = QUERY_HEADS // KEY_VALUE_HEADS
    prompt_key_input = jax.random.truncated_normal(jax.random.fold_in(key, 11), -5.0, 5.0, (PROMPT_TOKENS, KEY_VALUE_HEADS, HEAD_SIZE), jnp.float32)
    prompt_query_input = jax.random.truncated_normal(jax.random.fold_in(key, 12), -5.0, 5.0, (PROMPT_TOKENS, KEY_VALUE_HEADS, query_group_count, HEAD_SIZE), jnp.float32)
    response_key_input = jax.random.truncated_normal(jax.random.fold_in(key, 13), -5.0, 5.0, (2, RESPONSE_TOKENS, KEY_VALUE_HEADS, HEAD_SIZE), jnp.float32)
    response_query_input = jax.random.truncated_normal(jax.random.fold_in(key, 14), -5.0, 5.0, (2, RESPONSE_TOKENS, KEY_VALUE_HEADS, query_group_count, HEAD_SIZE), jnp.float32)
    return (prompt_query_input.reshape(PROMPT_TOKENS, QUERY_HEADS * HEAD_SIZE), prompt_key_input.reshape(PROMPT_TOKENS, KEY_VALUE_HEADS * HEAD_SIZE), response_query_input.reshape(2, RESPONSE_TOKENS, QUERY_HEADS * HEAD_SIZE), response_key_input.reshape(2, RESPONSE_TOKENS, KEY_VALUE_HEADS * HEAD_SIZE))


def draw_prompt_queries(key, part):
    return joint_draw(key)[0].astype(jnp.bfloat16)


def draw_prompt_key_rows(key, part):
    return joint_draw(key)[1].astype(jnp.bfloat16)


def draw_answer_queries(key, part):
    return joint_draw(key)[2].astype(jnp.bfloat16)


def draw_response_key_rows(key, part):
    return joint_draw(key)[3].astype(jnp.bfloat16)


def block_levels(own_key, shape, pieces, least, high):
    def one(axis_at, blocks):
        draws = jax.random.uniform(jax.random.fold_in(jax.random.fold_in(own_key, 6), axis_at), (blocks,), jnp.float32, least / len(pieces), high / len(pieces))
        return jnp.repeat(jnp.exp(draws), shape[axis_at] // blocks).reshape((-1,) + (1,) * (len(shape) - axis_at - 1))

    gain = one(*pieces[0])
    for cut in pieces[1:]:
        gain = gain * one(*cut)
    return gain


def gaussian(key, extent, spread, most, pieces=(), kind=jnp.bfloat16):
    loudness = block_levels(key, extent, pieces, -0.22, 0.18) if pieces else 1.0
    drawn = jax.random.normal(key, extent, jnp.float32) * spread * loudness
    return jnp.minimum(jnp.maximum(drawn, -most), most).astype(kind)


def setup_inputs(seed: int = 0) -> dict:
    seeds = jax.random.split(jax.random.key(seed), 11)
    return {
        "prompt_queries": draw_prompt_queries(jax.random.fold_in(seeds[10], 71), 0),
        "prompt_key_rows": draw_prompt_key_rows(jax.random.fold_in(seeds[10], 71), 0),
        "prompt_value_rows": gaussian(seeds[2], (PROMPT_TOKENS, KEY_VALUE_HEADS * HEAD_SIZE), 1.0, 6.0, ((0, 32), (1, 8))),
        "answer_queries": draw_answer_queries(jax.random.fold_in(seeds[10], 71), 0),
        "response_key_rows": draw_response_key_rows(jax.random.fold_in(seeds[10], 71), 0),
        "response_value_rows": gaussian(seeds[5], (2, RESPONSE_TOKENS, KEY_VALUE_HEADS * HEAD_SIZE), 1.0, 6.0, ((0, 2), (1, 16), (2, 8))),
        "prompt_cotangent": gaussian(seeds[6], (PROMPT_TOKENS, QUERY_HEADS * HEAD_SIZE), 1.0, 6.0, ((0, 32), (1, 8))),
        "answer_cotangent": gaussian(seeds[7], (2, RESPONSE_TOKENS, QUERY_HEADS * HEAD_SIZE), 1.0, 6.0, ((0, 2), (1, 16), (2, 8))),
        "prompt_length": jax.random.randint(seeds[8], (1,), PROMPT_TOKENS // 2 + 1, PROMPT_TOKENS + 1).astype(jnp.int32),
        "answer_lengths": jax.random.randint(seeds[9], (2,), RESPONSE_TOKENS // 2 + 1, RESPONSE_TOKENS + 1).astype(jnp.int32),
    }


NEGATIVE = -1.0e30


def attend(queries, cotangent, key_rows, value_rows, allowed, valid_rows, scaling):
    scores = jnp.dot(queries, key_rows.T, preferred_element_type=jnp.float32) * scaling
    scores = jnp.where(allowed, scores, NEGATIVE)
    row_max = jnp.max(scores, axis=1, keepdims=True)
    terms = jnp.where(allowed, jnp.exp(scores - row_max), 0.0)
    totals = jnp.sum(terms, axis=1, keepdims=True)
    log_total = row_max + jnp.log(totals)
    probs = terms.astype(jnp.bfloat16)
    output = jnp.dot(probs, value_rows, preferred_element_type=jnp.float32) / totals
    shares = jnp.where(allowed, jnp.exp(scores - log_total), 0.0)
    weights = shares.astype(jnp.bfloat16)
    attended = jnp.where(valid_rows[:, None], output, 0.0).astype(jnp.bfloat16)
    masked = jnp.where(valid_rows[:, None], cotangent, jnp.zeros_like(cotangent))
    row_delta = jnp.sum(masked.astype(jnp.float32) * output, axis=1, keepdims=True)
    prob_grad = jnp.dot(masked, value_rows.T, preferred_element_type=jnp.float32)
    score_grad = (shares * (prob_grad - row_delta)).astype(jnp.bfloat16)
    query_grad = (jnp.dot(score_grad, key_rows, preferred_element_type=jnp.float32) * scaling).astype(jnp.bfloat16)
    key_grad = jnp.dot(score_grad.T, queries, preferred_element_type=jnp.float32) * scaling
    value_grad = jnp.dot(weights.T, masked, preferred_element_type=jnp.float32)
    return attended, query_grad, key_grad, value_grad


def reference(prompt_queries, prompt_key_rows, prompt_value_rows, answer_queries, response_key_rows, response_value_rows, prompt_cotangent, answer_cotangent, prompt_length, answer_lengths):
    query_group_count = QUERY_HEADS // KEY_VALUE_HEADS
    scaling = HEAD_SIZE ** -0.5
    prompt_len = prompt_length[0]
    prompt_pos = jnp.arange(PROMPT_TOKENS, dtype=jnp.int32)
    answer_pos = jnp.arange(RESPONSE_TOKENS, dtype=jnp.int32)
    prompt_query_heads = prompt_queries.reshape(PROMPT_TOKENS, QUERY_HEADS, HEAD_SIZE).transpose(1, 0, 2)
    prompt_cot_heads = prompt_cotangent.reshape(PROMPT_TOKENS, QUERY_HEADS, HEAD_SIZE).transpose(1, 0, 2)
    answer_query_heads = answer_queries.reshape(2, RESPONSE_TOKENS, QUERY_HEADS, HEAD_SIZE).transpose(2, 0, 1, 3)
    answer_cot_heads = answer_cotangent.reshape(2, RESPONSE_TOKENS, QUERY_HEADS, HEAD_SIZE).transpose(2, 0, 1, 3)
    prompt_key_per_head = prompt_key_rows.reshape(PROMPT_TOKENS, KEY_VALUE_HEADS, HEAD_SIZE).transpose(1, 0, 2)
    prompt_value_per_head = prompt_value_rows.reshape(PROMPT_TOKENS, KEY_VALUE_HEADS, HEAD_SIZE).transpose(1, 0, 2)
    response_key_per_head = response_key_rows.reshape(2, RESPONSE_TOKENS, KEY_VALUE_HEADS, HEAD_SIZE).transpose(2, 0, 1, 3)
    response_value_per_head = response_value_rows.reshape(2, RESPONSE_TOKENS, KEY_VALUE_HEADS, HEAD_SIZE).transpose(2, 0, 1, 3)
    head_owner = jnp.arange(QUERY_HEADS, dtype=jnp.int32) // query_group_count
    causal = (prompt_pos[None, :] <= prompt_pos[:, None]) & (prompt_pos[None, :] < prompt_len)
    seen_prompt = jnp.broadcast_to((prompt_pos < prompt_len)[None, :], (RESPONSE_TOKENS, PROMPT_TOKENS))

    def per_head(inputs):
        queries, cotangent, later_queries, later_cot, owner = inputs
        key_rows = prompt_key_per_head[owner]
        value_rows = prompt_value_per_head[owner]
        first = attend(queries, cotangent, key_rows, value_rows, causal, prompt_pos < prompt_len, scaling)
        key_grad = first[2]
        value_grad = first[3]
        later = []
        for which in range(2):
            answer_len = answer_lengths[which]
            inner = (answer_pos[None, :] <= answer_pos[:, None]) & (answer_pos[None, :] < answer_len)
            joined_keys = jnp.concatenate([key_rows, response_key_per_head[owner, which]], axis=0)
            joined_values = jnp.concatenate([value_rows, response_value_per_head[owner, which]], axis=0)
            joined_allowed = jnp.concatenate([seen_prompt, inner], axis=1)
            result = attend(later_queries[which], later_cot[which], joined_keys, joined_values, joined_allowed, answer_pos < answer_len, scaling)
            key_grad = key_grad + result[2][:PROMPT_TOKENS]
            value_grad = value_grad + result[3][:PROMPT_TOKENS]
            later.append(result)
        answer_out = jnp.stack([later[0][0], later[1][0]])
        answer_qgrad = jnp.stack([later[0][1], later[1][1]])
        answer_kgrad = jnp.stack([later[0][2][PROMPT_TOKENS:], later[1][2][PROMPT_TOKENS:]])
        answer_vgrad = jnp.stack([later[0][3][PROMPT_TOKENS:], later[1][3][PROMPT_TOKENS:]])
        return first[0], first[1], key_grad, value_grad, answer_out, answer_qgrad, answer_kgrad, answer_vgrad

    output_collection = lax.map(per_head, (prompt_query_heads, prompt_cot_heads, answer_query_heads, answer_cot_heads, head_owner))
    prompt_attended = output_collection[0].transpose(1, 0, 2).reshape(PROMPT_TOKENS, QUERY_HEADS * HEAD_SIZE)
    prompt_query_grad = output_collection[1].transpose(1, 0, 2).reshape(PROMPT_TOKENS, QUERY_HEADS * HEAD_SIZE)
    prompt_key_gradient = output_collection[2].reshape(KEY_VALUE_HEADS, query_group_count, PROMPT_TOKENS, HEAD_SIZE).sum(axis=1).transpose(1, 0, 2).reshape(PROMPT_TOKENS, KEY_VALUE_HEADS * HEAD_SIZE).astype(jnp.bfloat16)
    prompt_value_gradient = output_collection[3].reshape(KEY_VALUE_HEADS, query_group_count, PROMPT_TOKENS, HEAD_SIZE).sum(axis=1).transpose(1, 0, 2).reshape(PROMPT_TOKENS, KEY_VALUE_HEADS * HEAD_SIZE).astype(jnp.bfloat16)
    answer_attended = output_collection[4].transpose(1, 2, 0, 3).reshape(2, RESPONSE_TOKENS, QUERY_HEADS * HEAD_SIZE)
    answer_query_grad = output_collection[5].transpose(1, 2, 0, 3).reshape(2, RESPONSE_TOKENS, QUERY_HEADS * HEAD_SIZE)
    response_key_gradient = output_collection[6].reshape(KEY_VALUE_HEADS, query_group_count, 2, RESPONSE_TOKENS, HEAD_SIZE).sum(axis=1).transpose(1, 2, 0, 3).reshape(2, RESPONSE_TOKENS, KEY_VALUE_HEADS * HEAD_SIZE).astype(jnp.bfloat16)
    response_value_gradient = output_collection[7].reshape(KEY_VALUE_HEADS, query_group_count, 2, RESPONSE_TOKENS, HEAD_SIZE).sum(axis=1).transpose(1, 2, 0, 3).reshape(2, RESPONSE_TOKENS, KEY_VALUE_HEADS * HEAD_SIZE).astype(jnp.bfloat16)
    return (prompt_attended, answer_attended, prompt_query_grad, prompt_key_gradient, prompt_value_gradient, answer_query_grad, response_key_gradient, response_value_gradient)
```

```python
import jax
import jax.numpy as jnp
from jax import lax
from jax.experimental import pallas as pl
from jax.experimental.pallas import tpu as pltpu
from jax.sharding import PartitionSpec as P

QUERY_HEADS = 64
KEY_VALUE_HEADS = 8
GROUP = QUERY_HEADS // KEY_VALUE_HEADS
HEAD_SIZE = 128
NEGATIVE = -1e30
SCALING = HEAD_SIZE ** (-0.5)
LOG2E = 1.4426950408889634
TO_LOG2 = SCALING * LOG2E
CHUNK = 256
F32 = jnp.float32
BF16 = jnp.bfloat16
VMEM = pl.BlockSpec(memory_space=pltpu.VMEM)
SMEM = pl.BlockSpec(memory_space=pltpu.SMEM)
KEYS, VALUES = slice(0, HEAD_SIZE), slice(HEAD_SIZE, 2 * HEAD_SIZE)


def dot(a, b, ca, cb):
    return lax.dot_general(a, b, (((ca,), (cb,)), ((), ())), preferred_element_type=F32)


def at(chunk):
    return pl.ds(pl.multiple_of(chunk * CHUNK, CHUNK), CHUNK)


def chunks_of(count):
    return lax.div(count + (CHUNK - 1), CHUNK)


def head(h):
    return slice(h * HEAD_SIZE, (h + 1) * HEAD_SIZE)


class Place:
    def __init__(self, place, rows, half):
        pair, ctx, prompt_len, self.answer_len = (place[i] for i in range(4))
        self.first = ctx * rows
        self.prompt_first = pair * half + self.first
        self.prompt_len = prompt_len
        self.own_len = jnp.clip(prompt_len - pair * half, 1, half)
        self.other_len = jnp.clip(prompt_len - (1 - pair) * half, 1, half)
        self.own_chunks = chunks_of(self.own_len)
        self.other_chunks = chunks_of(self.other_len)
        self.answer_chunks = jnp.where(
            self.first < self.answer_len, chunks_of(self.first + rows), 0
        )
        lane = lax.broadcasted_iota(jnp.int32, (1, rows * GROUP), 1)
        causal = self.first + lax.rem(lane, rows)
        flat = jnp.zeros_like(causal)
        self.own_limit = jnp.concatenate([causal, flat + (self.own_len - 1)], axis=1)
        self.other_limit = jnp.concatenate(
            [flat + jnp.where(pair > 0, half, -1), flat + (self.other_len - 1)], axis=1
        )
        self.answer_limit = causal


def prepare_kernel(place, prompt_q, answer_q, prompt_do, answer_do, q_t, do_t, both_s, *, half):
    rows = prompt_q.shape[0]
    lanes = rows * GROUP
    where = Place(place, rows, half)
    for k, (q_ref, do_ref, first, length) in enumerate(
        (
            (prompt_q, prompt_do, where.prompt_first, where.prompt_len),
            (answer_q, answer_do, where.first, where.answer_len),
        )
    ):
        live = first + lax.broadcasted_iota(jnp.int32, (rows, HEAD_SIZE), 0) < length
        q_rows = jnp.concatenate([q_ref[:, head(h)] for h in range(GROUP)], axis=0)
        do_rows = jnp.concatenate(
            [
                jnp.where(live, do_ref[:, head(h)].astype(F32), 0.0).astype(BF16)
                for h in range(GROUP)
            ],
            axis=0,
        )
        side = slice(k * lanes, (k + 1) * lanes)
        both_s[side, KEYS] = q_rows
        both_s[side, VALUES] = do_rows
        q_t[:, side] = q_rows.T
        do_t[:, side] = do_rows.T


def block_of(kv, c, part, cols):
    rows = part.stop - part.start
    count = CHUNK // rows
    return kv[pl.ds(c * count, count), part, cols].reshape(CHUNK, HEAD_SIZE)


def put_block(dkv, c, part, dk, dv):
    rows = part.stop - part.start
    count = CHUNK // rows
    dkv[pl.ds(c * count, count), part, KEYS] = dk.astype(BF16).reshape(count, rows, HEAD_SIZE)
    dkv[pl.ds(c * count, count), part, VALUES] = dv.astype(BF16).reshape(count, rows, HEAD_SIZE)


def masked_scores(kv, c, part, q_t, limit):
    s = dot(block_of(kv, c, part, KEYS), q_t, 1, 0)
    key = lax.broadcasted_iota(jnp.int32, s.shape, 0)
    return jnp.where(key <= limit - c * CHUNK, s, NEGATIVE)


def score_pass(kv, part, q_t, side, limit, chunks, scores):
    def step(c, run):
        s = masked_scores(kv, c, part, q_t[:, side], limit)
        scores[at(c), :] = s
        for k in range(CHUNK // 8):
            run = jnp.maximum(run, s[k * 8 : (k + 1) * 8])
        return run

    start = jnp.full((8, side.stop - side.start), NEGATIVE, F32)
    return lax.fori_loop(0, chunks, step, start)


def value_pass(kv, part, side, row_max, chunks, scores, o_t):
    def step(c, sums):
        p = jnp.exp2(scores[at(c), :] * TO_LOG2 - row_max)
        for k in range(CHUNK // 8):
            sums = sums + p[k * 8 : (k + 1) * 8]
        scores[at(c), :] = p
        o_t[:, side] += dot(block_of(kv, c, part, VALUES), p.astype(BF16), 0, 0)
        return sums

    start = jnp.zeros((8, side.stop - side.start), F32)
    return jnp.sum(lax.fori_loop(0, chunks, step, start), axis=0, keepdims=True)


def gradients(kv, c, part, shares, side, do_t, both_s, delta, dkv, dq_t):
    dp = dot(block_of(kv, c, part, VALUES), do_t[:, side], 1, 0)
    ds = (shares * (dp - delta)).astype(BF16)
    put_block(
        dkv,
        c,
        part,
        dot(ds, both_s[side, KEYS], 1, 0) * SCALING,
        dot(shares.astype(BF16), both_s[side, VALUES], 1, 0),
    )
    dq_t[:, side] += dot(block_of(kv, c, part, KEYS), ds, 0, 0)


def blank(dkv, part, begin):
    def step(c, _):
        zero = jnp.zeros((CHUNK, HEAD_SIZE), F32)
        put_block(dkv, c, part, zero, zero)
        return 0

    lax.fori_loop(begin, dkv.shape[0] * (part.stop - part.start) // CHUNK, step, 0)


def write_rows(ref, block_t, rows, first=None, length=None):
    block = block_t.T
    for h in range(GROUP):
        piece = block[h * rows : (h + 1) * rows]
        if first is not None:
            live = first + lax.broadcasted_iota(jnp.int32, (rows, HEAD_SIZE), 0) < length
            piece = jnp.where(live, piece, 0.0)
        ref[:, head(h)] = piece.astype(BF16)


def sides(q_t):
    lanes = q_t.shape[1] // 2
    return slice(0, lanes), slice(lanes, 2 * lanes), slice(0, 2 * lanes)


def own_forward_kernel(place, q_t, kv, o_t, stats, shared, own):
    rows = kv.shape[1] // 2
    prompt, answer, every = sides(q_t)
    where = Place(place, rows, kv.shape[0] * rows)
    upper, lower = slice(0, rows), slice(rows, 2 * rows)
    run = score_pass(kv, upper, q_t, every, where.own_limit, where.own_chunks, shared)
    own_run = score_pass(kv, lower, q_t, answer, where.answer_limit, where.answer_chunks, own)
    run = jnp.concatenate([run[:, prompt], jnp.maximum(run[:, answer], own_run)], axis=1)
    row_max = jnp.max(run, axis=0, keepdims=True) * TO_LOG2
    o_t[...] = jnp.zeros_like(o_t)
    total = value_pass(kv, upper, every, row_max, where.own_chunks, shared, o_t)
    own_total = value_pass(
        kv, lower, answer, row_max[:, answer], where.answer_chunks, own, o_t
    )
    stats[0:1, :] = row_max
    stats[1:2, prompt] = total[:, prompt]
    stats[1:2, answer] = total[:, answer] + own_total


def other_kernel(
    place, q_t, do_t, both_s, kv, o_in, stats, prompt_out, answer_out, dkv, dq_t, factors, scores, o_t
):
    rows = kv.shape[1]
    prompt, answer, every = sides(q_t)
    where = Place(place, rows, kv.shape[0] * rows)
    part = slice(0, rows)
    chunks = where.other_chunks
    run = score_pass(kv, part, q_t, every, where.other_limit, chunks, scores)
    own_max = stats[0:1, :]
    row_max = jnp.maximum(jnp.max(run, axis=0, keepdims=True) * TO_LOG2, own_max)
    shrink = jnp.exp2(own_max - row_max)
    o_t[...] = o_in[...] * shrink
    total = value_pass(kv, part, every, row_max, chunks, scores, o_t) + stats[1:2, :] * shrink
    inverse = 1.0 / total
    out_t = o_t[...] * inverse
    delta = jnp.sum(do_t[...].astype(F32) * out_t, axis=0, keepdims=True)
    factors[0:1, :] = row_max + jnp.log(total) * LOG2E
    factors[1:2, :] = delta
    write_rows(prompt_out, out_t[:, prompt], rows, where.prompt_first, where.prompt_len)
    write_rows(answer_out, out_t[:, answer], rows, where.first, where.answer_len)
    dq_t[...] = jnp.zeros_like(dq_t)

    def step(c, _):
        shares = scores[at(c), :] * inverse
        gradients(kv, c, part, shares, every, do_t, both_s, delta, dkv, dq_t)
        return 0

    lax.fori_loop(0, chunks, step, 0)
    blank(dkv, part, chunks)


def own_backward_kernel(
    place, q_t, do_t, both_s, kv, factors, dq_in, prompt_dq, answer_dq, dkv, dq_t
):
    rows = kv.shape[1] // 2
    prompt, answer, every = sides(q_t)
    where = Place(place, rows, kv.shape[0] * rows)
    dq_t[...] = dq_in[...]

    def run(part, side, limit, chunks):
        log_total, delta = factors[0:1, side], factors[1:2, side]

        def step(c, _):
            s = masked_scores(kv, c, part, q_t[:, side], limit)
            shares = jnp.exp2(s * TO_LOG2 - log_total)
            gradients(kv, c, part, shares, side, do_t, both_s, delta, dkv, dq_t)
            return 0

        lax.fori_loop(0, chunks, step, 0)
        blank(dkv, part, chunks)

    run(slice(0, rows), every, where.own_limit, where.own_chunks)
    run(slice(rows, 2 * rows), answer, where.answer_limit, where.answer_chunks)
    write_rows(prompt_dq, dq_t[:, prompt] * SCALING, rows)
    write_rows(answer_dq, dq_t[:, answer] * SCALING, rows)


def call(kernel, name, arrays, outs, scratch, flops, mib):
    return pl.pallas_call(
        kernel,
        out_shape=[jax.ShapeDtypeStruct(*o) for o in outs],
        in_specs=[SMEM] + [VMEM] * (len(arrays) - 1),
        out_specs=[VMEM] * len(outs),
        scratch_shapes=[pltpu.VMEM(*s) for s in scratch],
        compiler_params=pltpu.CompilerParams(vmem_limit_bytes=mib * 1024 * 1024),
        cost_estimate=pl.CostEstimate(flops=flops, bytes_accessed=0, transcendentals=0),
        name=name,
    )(*arrays)


def copies_of(parts, count):
    rows = parts[0].shape[0]

    def kernel(pk, pv, ak, av, out, alone):
        alone[:, KEYS] = pk[...]
        alone[:, VALUES] = pv[...]
        for i in range(count):
            out[i, :rows, KEYS] = pk[...]
            out[i, :rows, VALUES] = pv[...]
            out[i, rows:, KEYS] = ak[...]
            out[i, rows:, VALUES] = av[...]

    return pl.pallas_call(
        kernel,
        out_shape=[
            jax.ShapeDtypeStruct((count, 2 * rows, 2 * HEAD_SIZE), BF16),
            jax.ShapeDtypeStruct((rows, 2 * HEAD_SIZE), BF16),
        ],
        in_specs=[VMEM] * 4,
        out_specs=[VMEM] * 2,
        compiler_params=pltpu.CompilerParams(vmem_limit_bytes=67043328),
        cost_estimate=pl.CostEstimate(flops=10**6, bytes_accessed=0, transcendentals=0),
        name="copies",
    )(*parts)


def exchanged(pieces):
    return lax.all_to_all(pieces, "ctx", split_axis=0, concat_axis=0, tiled=True)


def to_partner(block):
    count = lax.axis_size("pair")
    return lax.ppermute(block, "pair", [(i, count - 1 - i) for i in range(count)])


def body(
    prompt_queries,
    prompt_key_rows,
    prompt_value_rows,
    answer_queries,
    response_key_rows,
    response_value_rows,
    prompt_cotangent,
    answer_cotangent,
    prompt_length,
    answer_lengths,
):
    rows = prompt_queries.shape[0]
    lanes = rows * GROUP
    pair_index = lax.axis_index("pair")
    count = lax.axis_size("ctx")
    half = count * rows
    copies, alone = copies_of(
        (prompt_key_rows, prompt_value_rows, response_key_rows[0], response_value_rows[0]), count
    )
    own_kv = exchanged(copies)
    other = to_partner(alone)
    other_copies = jnp.broadcast_to(other[None], (count, *other.shape))
    place = jnp.stack(
        [
            pair_index,
            lax.axis_index("ctx"),
            prompt_length[0],
            lax.dynamic_index_in_dim(answer_lengths, pair_index, keepdims=False),
        ]
    ).astype(jnp.int32)
    wide, tall = (HEAD_SIZE, 2 * lanes), (2 * lanes, 2 * HEAD_SIZE)
    out = ((rows, GROUP * HEAD_SIZE), BF16)
    stat = ((8, 2 * lanes), F32)
    q_t, do_t, both_s = call(
        lambda *refs: prepare_kernel(*refs, half=half),
        "prepare",
        (place, prompt_queries, answer_queries[0], prompt_cotangent, answer_cotangent[0]),
        [(wide, BF16), (wide, BF16), (tall, BF16)],
        [],
        10**9,
        8,
    )
    own_kv, other_copies, q_t, do_t, both_s = lax.optimization_barrier(
        (own_kv, other_copies, q_t, do_t, both_s)
    )
    other_kv = exchanged(other_copies)
    flops = 2 * half * lanes * HEAD_SIZE
    o_t, stats = call(
        own_forward_kernel,
        "own_forward",
        (place, q_t, own_kv),
        [(wide, F32), stat],
        [((half, 2 * lanes), F32), ((half, lanes), F32)],
        8 * flops,
        16,
    )
    prompt_out, answer_out, other_dkv, dq_t, factors = call(
        other_kernel,
        "other",
        (place, q_t, do_t, both_s, other_kv, o_t, stats),
        [out, out, (other_kv.shape, BF16), (wide, F32), stat],
        [((half, 2 * lanes), F32), (wide, F32)],
        12 * flops,
        16,
    )
    other_sum = exchanged(other_dkv).astype(F32).sum(axis=0)
    prompt_dq, answer_dq, own_dkv = call(
        own_backward_kernel,
        "own_backward",
        (place, q_t, do_t, both_s, own_kv, factors, dq_t),
        [out, out, (own_kv.shape, BF16)],
        [(wide, F32)],
        18 * flops,
        16,
    )
    from_partner = to_partner(other_sum)
    own_sum = exchanged(own_dkv).astype(F32).sum(axis=0)
    prompt_grad = (own_sum[:rows] + from_partner).astype(BF16)
    answer_grad = own_sum[rows:].astype(BF16)
    return (
        prompt_out,
        answer_out[None],
        prompt_dq,
        prompt_grad[:, KEYS],
        prompt_grad[:, VALUES],
        answer_dq[None],
        answer_grad[None, :, KEYS],
        answer_grad[None, :, VALUES],
    )


def solution(mesh):
    prompt = P(("pair", "ctx"), "head")
    answer = P("pair", "ctx", "head")
    return jax.shard_map(
        body,
        mesh=mesh,
        in_specs=(prompt, prompt, prompt, answer, answer, answer, prompt, answer, P(), P()),
        out_specs=(prompt, answer, prompt, prompt, prompt, answer, answer, answer),
        check_vma=False,
    )
```

```python
import jax
import jax.numpy as jnp
from jax import lax
from jax.experimental import pallas as pl
from jax.experimental.pallas import tpu as pltpu
from jax.sharding import PartitionSpec as P

QUERY_HEADS = 64
KEY_VALUE_HEADS = 8
GROUP = QUERY_HEADS // KEY_VALUE_HEADS
HEAD_SIZE = 128
NEGATIVE = -1e30
SCALING = HEAD_SIZE ** (-0.5)
LOG2E = 1.4426950408889634
TO_LOG2 = SCALING * LOG2E
CHUNK = 256
F32 = jnp.float32
BF16 = jnp.bfloat16
VMEM = pl.BlockSpec(memory_space=pltpu.VMEM)
SMEM = pl.BlockSpec(memory_space=pltpu.SMEM)
KEYS, VALUES = slice(0, HEAD_SIZE), slice(HEAD_SIZE, 2 * HEAD_SIZE)


def dot(a, b, ca, cb):
    return lax.dot_general(a, b, (((ca,), (cb,)), ((), ())), preferred_element_type=F32)


def at(chunk):
    return pl.ds(pl.multiple_of(chunk * CHUNK, CHUNK), CHUNK)


def chunks_of(count):
    return lax.div(count + (CHUNK - 1), CHUNK)


def head(h):
    return slice(h * HEAD_SIZE, (h + 1) * HEAD_SIZE)


class Place:
    def __init__(self, place, rows, half):
        pair, ctx, prompt_len, self.answer_len = (place[i] for i in range(4))
        self.first = ctx * rows
        self.prompt_first = pair * half + self.first
        self.prompt_len = prompt_len
        self.own_len = jnp.clip(prompt_len - pair * half, 1, half)
        self.other_len = jnp.clip(prompt_len - (1 - pair) * half, 1, half)
        self.own_chunks = chunks_of(self.own_len)
        self.other_chunks = chunks_of(self.other_len)
        self.answer_chunks = jnp.where(
            self.first < self.answer_len, chunks_of(self.first + rows), 0
        )
        lane = lax.broadcasted_iota(jnp.int32, (1, rows * GROUP), 1)
        causal = self.first + lax.rem(lane, rows)
        flat = jnp.zeros_like(causal)
        self.own_limit = jnp.concatenate([causal, flat + (self.own_len - 1)], axis=1)
        self.other_limit = jnp.concatenate(
            [flat + jnp.where(pair > 0, half, -1), flat + (self.other_len - 1)], axis=1
        )
        self.answer_limit = causal


def prepare_kernel(
    place,
    prompt_q,
    answer_q,
    prompt_do,
    answer_do,
    answer_k,
    answer_v,
    q_t,
    do_t,
    both_s,
    answer_copies,
    *,
    half,
):
    rows = prompt_q.shape[0]
    for i in range(answer_copies.shape[0]):
        answer_copies[i, :, KEYS] = answer_k[...]
        answer_copies[i, :, VALUES] = answer_v[...]
    lanes = rows * GROUP
    where = Place(place, rows, half)
    for k, (q_ref, do_ref, first, length) in enumerate(
        (
            (prompt_q, prompt_do, where.prompt_first, where.prompt_len),
            (answer_q, answer_do, where.first, where.answer_len),
        )
    ):
        live = first + lax.broadcasted_iota(jnp.int32, (rows, HEAD_SIZE), 0) < length
        q_rows = jnp.concatenate([q_ref[:, head(h)] for h in range(GROUP)], axis=0)
        do_rows = jnp.concatenate(
            [
                jnp.where(live, do_ref[:, head(h)].astype(F32), 0.0).astype(BF16)
                for h in range(GROUP)
            ],
            axis=0,
        )
        side = slice(k * lanes, (k + 1) * lanes)
        both_s[side, KEYS] = q_rows
        both_s[side, VALUES] = do_rows
        q_t[:, side] = q_rows.T
        do_t[:, side] = do_rows.T


def block_of(kv, c, part, cols):
    rows = part.stop - part.start
    count = CHUNK // rows
    return kv[pl.ds(c * count, count), part, cols].reshape(CHUNK, HEAD_SIZE)


def put_block(dkv, c, part, dk, dv):
    rows = part.stop - part.start
    count = CHUNK // rows
    dkv[pl.ds(c * count, count), part, KEYS] = dk.astype(BF16).reshape(count, rows, HEAD_SIZE)
    dkv[pl.ds(c * count, count), part, VALUES] = dv.astype(BF16).reshape(count, rows, HEAD_SIZE)


def masked_scores(kv, c, part, q_t, limit):
    s = dot(block_of(kv, c, part, KEYS), q_t, 1, 0)
    key = lax.broadcasted_iota(jnp.int32, s.shape, 0)
    return jnp.where(key <= limit - c * CHUNK, s, NEGATIVE)


def score_pass(kv, part, q_t, side, limit, chunks, scores):
    def step(c, run):
        s = masked_scores(kv, c, part, q_t[:, side], limit)
        scores[at(c), :] = s
        for k in range(CHUNK // 8):
            run = jnp.maximum(run, s[k * 8 : (k + 1) * 8])
        return run

    start = jnp.full((8, side.stop - side.start), NEGATIVE, F32)
    return lax.fori_loop(0, chunks, step, start)


def value_pass(kv, part, side, row_max, chunks, scores, o_t):
    def step(c, sums):
        p = jnp.exp2(scores[at(c), :] * TO_LOG2 - row_max)
        for k in range(CHUNK // 8):
            sums = sums + p[k * 8 : (k + 1) * 8]
        scores[at(c), :] = p
        o_t[:, side] += dot(block_of(kv, c, part, VALUES), p.astype(BF16), 0, 0)
        return sums

    start = jnp.zeros((8, side.stop - side.start), F32)
    return jnp.sum(lax.fori_loop(0, chunks, step, start), axis=0, keepdims=True)


def gradients(kv, c, part, shares, side, do_t, both_s, delta, dkv, out_part, dq_t):
    dp = dot(block_of(kv, c, part, VALUES), do_t[:, side], 1, 0)
    ds = (shares * (dp - delta)).astype(BF16)
    put_block(
        dkv,
        c,
        out_part,
        dot(ds, both_s[side, KEYS], 1, 0) * SCALING,
        dot(shares.astype(BF16), both_s[side, VALUES], 1, 0),
    )
    dq_t[:, side] += dot(block_of(kv, c, part, KEYS), ds, 0, 0)


def blank(dkv, part, begin):
    def step(c, _):
        zero = jnp.zeros((CHUNK, HEAD_SIZE), F32)
        put_block(dkv, c, part, zero, zero)
        return 0

    lax.fori_loop(begin, dkv.shape[0] * (part.stop - part.start) // CHUNK, step, 0)


def write_rows(ref, block_t, rows, first=None, length=None):
    block = block_t.T
    for h in range(GROUP):
        piece = block[h * rows : (h + 1) * rows]
        if first is not None:
            live = first + lax.broadcasted_iota(jnp.int32, (rows, HEAD_SIZE), 0) < length
            piece = jnp.where(live, piece, 0.0)
        ref[:, head(h)] = piece.astype(BF16)


def sides(q_t):
    lanes = q_t.shape[1] // 2
    return slice(0, lanes), slice(lanes, 2 * lanes), slice(0, 2 * lanes)


def own_forward_kernel(place, q_t, kv, o_t, stats, scores):
    rows = kv.shape[1]
    every = sides(q_t)[2]
    where = Place(place, rows, kv.shape[0] * rows)
    part = slice(0, rows)
    run = score_pass(kv, part, q_t, every, where.own_limit, where.own_chunks, scores)
    row_max = jnp.max(run, axis=0, keepdims=True) * TO_LOG2
    o_t[...] = jnp.zeros_like(o_t)
    stats[0:1, :] = row_max
    stats[1:2, :] = value_pass(kv, part, every, row_max, where.own_chunks, scores, o_t)


def other_kernel(
    place,
    q_t,
    do_t,
    both_s,
    kv,
    answer_kv,
    o_in,
    stats,
    prompt_out,
    answer_out,
    dkv,
    dq_t,
    factors,
    scores,
    answer_scores,
    o_t,
):
    rows = kv.shape[1]
    prompt, answer, every = sides(q_t)
    where = Place(place, rows, kv.shape[0] * rows)
    part = slice(0, rows)
    chunks = where.other_chunks
    run = score_pass(kv, part, q_t, every, where.other_limit, chunks, scores)
    answer_run = score_pass(
        answer_kv, part, q_t, answer, where.answer_limit, where.answer_chunks, answer_scores
    )
    run = jnp.concatenate([run[:, prompt], jnp.maximum(run[:, answer], answer_run)], axis=1)
    own_max = stats[0:1, :]
    row_max = jnp.maximum(jnp.max(run, axis=0, keepdims=True) * TO_LOG2, own_max)
    shrink = jnp.exp2(own_max - row_max)
    o_t[...] = o_in[...] * shrink
    total = value_pass(kv, part, every, row_max, chunks, scores, o_t) + stats[1:2, :] * shrink
    answer_total = value_pass(
        answer_kv, part, answer, row_max[:, answer], where.answer_chunks, answer_scores, o_t
    )
    total = jnp.concatenate([total[:, prompt], total[:, answer] + answer_total], axis=1)
    inverse = 1.0 / total
    out_t = o_t[...] * inverse
    delta = jnp.sum(do_t[...].astype(F32) * out_t, axis=0, keepdims=True)
    factors[0:1, :] = row_max + jnp.log(total) * LOG2E
    factors[1:2, :] = delta
    write_rows(prompt_out, out_t[:, prompt], rows, where.prompt_first, where.prompt_len)
    write_rows(answer_out, out_t[:, answer], rows, where.first, where.answer_len)
    dq_t[...] = jnp.zeros_like(dq_t)

    def step(c, _):
        shares = scores[at(c), :] * inverse
        gradients(kv, c, part, shares, every, do_t, both_s, delta, dkv, part, dq_t)
        return 0

    lax.fori_loop(0, chunks, step, 0)
    blank(dkv, part, chunks)


def own_backward_kernel(
    place, q_t, do_t, both_s, kv, answer_kv, factors, dq_in, prompt_dq, answer_dq, dkv, dq_t
):
    rows = kv.shape[1]
    prompt, answer, every = sides(q_t)
    where = Place(place, rows, kv.shape[0] * rows)
    part = slice(0, rows)
    dq_t[...] = dq_in[...]

    def run(kv, out_part, side, limit, chunks):
        log_total, delta = factors[0:1, side], factors[1:2, side]

        def step(c, _):
            s = masked_scores(kv, c, part, q_t[:, side], limit)
            shares = jnp.exp2(s * TO_LOG2 - log_total)
            gradients(kv, c, part, shares, side, do_t, both_s, delta, dkv, out_part, dq_t)
            return 0

        lax.fori_loop(0, chunks, step, 0)
        blank(dkv, out_part, chunks)

    run(kv, part, every, where.own_limit, where.own_chunks)
    run(answer_kv, slice(rows, 2 * rows), answer, where.answer_limit, where.answer_chunks)
    write_rows(prompt_dq, dq_t[:, prompt] * SCALING, rows)
    write_rows(answer_dq, dq_t[:, answer] * SCALING, rows)


def call(kernel, name, arrays, outs, scratch, flops, mib):
    return pl.pallas_call(
        kernel,
        out_shape=[jax.ShapeDtypeStruct(*o) for o in outs],
        in_specs=[SMEM] + [VMEM] * (len(arrays) - 1),
        out_specs=[VMEM] * len(outs),
        scratch_shapes=[pltpu.VMEM(*s) for s in scratch],
        compiler_params=pltpu.CompilerParams(vmem_limit_bytes=mib * 1024 * 1024),
        cost_estimate=pl.CostEstimate(flops=flops, bytes_accessed=0, transcendentals=0),
        name=name,
    )(*arrays)


def copies_of(keys, values, count):
    rows = keys.shape[0]

    def kernel(k, v, out):
        for i in range(count):
            out[i, :, KEYS] = k[...]
            out[i, :, VALUES] = v[...]

    return pl.pallas_call(
        kernel,
        out_shape=jax.ShapeDtypeStruct((count, rows, 2 * HEAD_SIZE), BF16),
        in_specs=[VMEM] * 2,
        out_specs=VMEM,
        compiler_params=pltpu.CompilerParams(vmem_limit_bytes=67043328),
        cost_estimate=pl.CostEstimate(flops=10**6, bytes_accessed=0, transcendentals=0),
        name="copies",
    )(keys, values)


def exchanged(pieces):
    return lax.all_to_all(pieces, "ctx", split_axis=0, concat_axis=0, tiled=True)


def to_partner(block):
    count = lax.axis_size("pair")
    return lax.ppermute(block, "pair", [(i, count - 1 - i) for i in range(count)])


def body(
    prompt_queries,
    prompt_key_rows,
    prompt_value_rows,
    answer_queries,
    response_key_rows,
    response_value_rows,
    prompt_cotangent,
    answer_cotangent,
    prompt_length,
    answer_lengths,
):
    rows = prompt_queries.shape[0]
    lanes = rows * GROUP
    pair_index = lax.axis_index("pair")
    count = lax.axis_size("ctx")
    half = count * rows
    own_kv = exchanged(copies_of(prompt_key_rows, prompt_value_rows, count))
    place = jnp.stack(
        [
            pair_index,
            lax.axis_index("ctx"),
            prompt_length[0],
            lax.dynamic_index_in_dim(answer_lengths, pair_index, keepdims=False),
        ]
    ).astype(jnp.int32)
    wide, tall = (HEAD_SIZE, 2 * lanes), (2 * lanes, 2 * HEAD_SIZE)
    out = ((rows, GROUP * HEAD_SIZE), BF16)
    stat = ((8, 2 * lanes), F32)
    kv_shape = (count, rows, 2 * HEAD_SIZE)
    q_t, do_t, both_s, answer_copies = call(
        lambda *refs: prepare_kernel(*refs, half=half),
        "prepare",
        (
            place,
            prompt_queries,
            answer_queries[0],
            prompt_cotangent,
            answer_cotangent[0],
            response_key_rows[0],
            response_value_rows[0],
        ),
        [(wide, BF16), (wide, BF16), (tall, BF16), (kv_shape, BF16)],
        [],
        10**9,
        8,
    )
    own_kv, answer_copies, q_t, do_t, both_s = lax.optimization_barrier(
        (own_kv, answer_copies, q_t, do_t, both_s)
    )
    other_kv = to_partner(own_kv)
    answer_kv = exchanged(answer_copies)
    flops = 2 * half * lanes * HEAD_SIZE
    o_t, stats = call(
        own_forward_kernel,
        "own_forward",
        (place, q_t, own_kv),
        [(wide, F32), stat],
        [((half, 2 * lanes), F32)],
        8 * flops,
        16,
    )
    prompt_out, answer_out, other_dkv, dq_t, factors = call(
        other_kernel,
        "other",
        (place, q_t, do_t, both_s, other_kv, answer_kv, o_t, stats),
        [out, out, (kv_shape, BF16), (wide, F32), stat],
        [((half, 2 * lanes), F32), ((half, lanes), F32), (wide, F32)],
        12 * flops,
        16,
    )
    other_sum = exchanged(other_dkv).astype(F32).sum(axis=0)
    prompt_dq, answer_dq, own_dkv = call(
        own_backward_kernel,
        "own_backward",
        (place, q_t, do_t, both_s, own_kv, answer_kv, factors, dq_t),
        [out, out, ((count, 2 * rows, 2 * HEAD_SIZE), BF16)],
        [(wide, F32)],
        18 * flops,
        16,
    )
    from_partner = to_partner(other_sum)
    own_sum = exchanged(own_dkv).astype(F32).sum(axis=0)
    prompt_grad = (own_sum[:rows] + from_partner).astype(BF16)
    answer_grad = own_sum[rows:].astype(BF16)
    return (
        prompt_out,
        answer_out[None],
        prompt_dq,
        prompt_grad[:, KEYS],
        prompt_grad[:, VALUES],
        answer_dq[None],
        answer_grad[None, :, KEYS],
        answer_grad[None, :, VALUES],
    )


def solution(mesh):
    prompt = P(("pair", "ctx"), "head")
    answer = P("pair", "ctx", "head")
    return jax.shard_map(
        body,
        mesh=mesh,
        in_specs=(prompt, prompt, prompt, answer, answer, answer, prompt, answer, P(), P()),
        out_specs=(prompt, answer, prompt, prompt, prompt, answer, answer, answer),
        check_vma=False,
    )
```

```python
import jax
import jax.numpy as jnp
from jax import lax
from jax.experimental import pallas as pl
from jax.experimental.pallas import tpu as pltpu
from jax.sharding import PartitionSpec as P

QUERY_HEADS = 64
KEY_VALUE_HEADS = 8
GROUP = QUERY_HEADS // KEY_VALUE_HEADS
HEAD_SIZE = 128
NEGATIVE = -1e30
SCALING = HEAD_SIZE ** (-0.5)
LOG2E = 1.4426950408889634
TO_LOG2 = SCALING * LOG2E
CHUNK = 256
F32 = jnp.float32
BF16 = jnp.bfloat16
VMEM = pl.BlockSpec(memory_space=pltpu.VMEM)
SMEM = pl.BlockSpec(memory_space=pltpu.SMEM)
KEYS, VALUES = slice(0, HEAD_SIZE), slice(HEAD_SIZE, 2 * HEAD_SIZE)


def dot(a, b, ca, cb):
    return lax.dot_general(a, b, (((ca,), (cb,)), ((), ())), preferred_element_type=F32)


def at(chunk):
    return pl.ds(pl.multiple_of(chunk * CHUNK, CHUNK), CHUNK)


def chunks_of(count):
    return lax.div(count + (CHUNK - 1), CHUNK)


def head(h):
    return slice(h * HEAD_SIZE, (h + 1) * HEAD_SIZE)


class Place:
    def __init__(self, place, rows, half):
        pair, ctx, prompt_len, self.answer_len = (place[i] for i in range(4))
        self.first = ctx * rows
        self.prompt_first = pair * half + self.first
        self.prompt_len = prompt_len
        self.own_len = jnp.clip(prompt_len - pair * half, 1, half)
        self.other_len = jnp.clip(prompt_len - (1 - pair) * half, 1, half)
        self.own_chunks = chunks_of(self.own_len)
        self.other_chunks = chunks_of(self.other_len)
        self.answer_chunks = jnp.where(
            self.first < self.answer_len, chunks_of(self.first + rows), 0
        )
        lane = lax.broadcasted_iota(jnp.int32, (1, rows * GROUP), 1)
        causal = self.first + lax.rem(lane, rows)
        flat = jnp.zeros_like(causal)
        self.own_limit = jnp.concatenate([causal, flat + (self.own_len - 1)], axis=1)
        self.other_limit = jnp.concatenate(
            [flat + jnp.where(pair > 0, half, -1), flat + (self.other_len - 1)], axis=1
        )
        self.answer_limit = causal


def prepare_kernel(
    place,
    prompt_q,
    answer_q,
    prompt_do,
    answer_do,
    answer_k,
    answer_v,
    q_t,
    both_s,
    answer_copies,
    *,
    half,
):
    rows = prompt_q.shape[0]
    for i in range(answer_copies.shape[0]):
        answer_copies[i, :, KEYS] = answer_k[...]
        answer_copies[i, :, VALUES] = answer_v[...]
    lanes = rows * GROUP
    where = Place(place, rows, half)
    for k, (q_ref, do_ref, first, length) in enumerate(
        (
            (prompt_q, prompt_do, where.prompt_first, where.prompt_len),
            (answer_q, answer_do, where.first, where.answer_len),
        )
    ):
        live = first + lax.broadcasted_iota(jnp.int32, (rows, HEAD_SIZE), 0) < length
        q_rows = jnp.concatenate([q_ref[:, head(h)] for h in range(GROUP)], axis=0)
        do_rows = jnp.concatenate(
            [
                jnp.where(live, do_ref[:, head(h)].astype(F32), 0.0).astype(BF16)
                for h in range(GROUP)
            ],
            axis=0,
        )
        side = slice(k * lanes, (k + 1) * lanes)
        both_s[side, KEYS] = q_rows
        both_s[side, VALUES] = do_rows
        q_t[:, side] = q_rows.T


def block_of(kv, c, part, cols):
    rows = part.stop - part.start
    count = CHUNK // rows
    return kv[pl.ds(c * count, count), part, cols].reshape(CHUNK, HEAD_SIZE)


def put_block(dkv, c, dk, dv):
    rows = dkv.shape[1]
    count = CHUNK // rows
    for cols, d in ((KEYS, dk), (VALUES, dv)):
        dkv[pl.ds(c * count, count), :, cols] = d.astype(dkv.dtype).reshape(count, rows, HEAD_SIZE)


def masked_scores(kv, c, part, q_t, limit):
    s = dot(block_of(kv, c, part, KEYS), q_t, 1, 0)
    key = lax.broadcasted_iota(jnp.int32, s.shape, 0)
    return jnp.where(key <= limit - c * CHUNK, s, NEGATIVE)


def score_pass(kv, part, q_t, side, limit, chunks, scores):
    def step(c, run):
        s = masked_scores(kv, c, part, q_t[:, side], limit)
        scores[at(c), :] = s
        for k in range(CHUNK // 8):
            run = jnp.maximum(run, s[k * 8 : (k + 1) * 8])
        return run

    start = jnp.full((8, side.stop - side.start), NEGATIVE, F32)
    return lax.fori_loop(0, chunks, step, start)


def value_pass(kv, part, side, row_max, chunks, scores, o_t):
    def step(c, sums):
        p = jnp.exp2(scores[at(c), :] * TO_LOG2 - row_max)
        for k in range(CHUNK // 8):
            sums = sums + p[k * 8 : (k + 1) * 8]
        scores[at(c), :] = p
        o_t[:, side] += dot(block_of(kv, c, part, VALUES), p.astype(BF16), 0, 0)
        return sums

    start = jnp.zeros((8, side.stop - side.start), F32)
    return jnp.sum(lax.fori_loop(0, chunks, step, start), axis=0, keepdims=True)


def gradients(kv, c, part, shares, side, do_t, both_s, delta, dkv, dq_t):
    dp = dot(block_of(kv, c, part, VALUES), do_t[:, side], 1, 0)
    ds = (shares * (dp - delta)).astype(BF16)
    put_block(
        dkv,
        c,
        dot(ds, both_s[side, KEYS], 1, 0) * SCALING,
        dot(shares.astype(BF16), both_s[side, VALUES], 1, 0),
    )
    dq_t[:, side] += dot(block_of(kv, c, part, KEYS), ds, 0, 0)


def blank(dkv, begin):
    def step(c, _):
        zero = jnp.zeros((CHUNK, HEAD_SIZE), F32)
        put_block(dkv, c, zero, zero)
        return 0

    lax.fori_loop(begin, dkv.shape[0] * dkv.shape[1] // CHUNK, step, 0)


def write_rows(ref, block_t, rows, first=None, length=None):
    block = block_t.T
    for h in range(GROUP):
        piece = block[h * rows : (h + 1) * rows]
        if first is not None:
            live = first + lax.broadcasted_iota(jnp.int32, (rows, HEAD_SIZE), 0) < length
            piece = jnp.where(live, piece, 0.0)
        ref[:, head(h)] = piece.astype(BF16)


def sides(q_t):
    lanes = q_t.shape[1] // 2
    return slice(0, lanes), slice(lanes, 2 * lanes), slice(0, 2 * lanes)


def own_forward_kernel(place, q_t, kv, o_t, stats, scores):
    rows = kv.shape[1]
    every = sides(q_t)[2]
    where = Place(place, rows, kv.shape[0] * rows)
    part = slice(0, rows)
    run = score_pass(kv, part, q_t, every, where.own_limit, where.own_chunks, scores)
    row_max = jnp.max(run, axis=0, keepdims=True) * TO_LOG2
    o_t[...] = jnp.zeros_like(o_t)
    stats[0:1, :] = row_max
    stats[1:2, :] = value_pass(kv, part, every, row_max, where.own_chunks, scores, o_t)


def other_kernel(
    place,
    q_t,
    both_s,
    kv,
    answer_kv,
    o_in,
    stats,
    prompt_out,
    answer_out,
    dkv,
    answer_dkv,
    dq_t,
    factors,
    scores,
    answer_scores,
    o_t,
    do_t,
):
    rows = kv.shape[1]
    prompt, answer, every = sides(q_t)
    where = Place(place, rows, kv.shape[0] * rows)
    part = slice(0, rows)
    chunks = where.other_chunks
    run = score_pass(kv, part, q_t, every, where.other_limit, chunks, scores)
    answer_run = score_pass(
        answer_kv, part, q_t, answer, where.answer_limit, where.answer_chunks, answer_scores
    )
    run = jnp.concatenate([run[:, prompt], jnp.maximum(run[:, answer], answer_run)], axis=1)
    do_t[...] = both_s[:, VALUES].T
    own_max = stats[0:1, :]
    row_max = jnp.maximum(jnp.max(run, axis=0, keepdims=True) * TO_LOG2, own_max)
    shrink = jnp.exp2(own_max - row_max)
    o_t[...] = o_in[...] * shrink
    total = value_pass(kv, part, every, row_max, chunks, scores, o_t) + stats[1:2, :] * shrink
    answer_total = value_pass(
        answer_kv, part, answer, row_max[:, answer], where.answer_chunks, answer_scores, o_t
    )
    total = jnp.concatenate([total[:, prompt], total[:, answer] + answer_total], axis=1)
    inverse = 1.0 / total
    out_t = o_t[...] * inverse
    delta = jnp.sum(do_t[...].astype(F32) * out_t, axis=0, keepdims=True)
    factors[0:1, :] = row_max + jnp.log(total) * LOG2E
    factors[1:2, :] = delta
    write_rows(prompt_out, out_t[:, prompt], rows, where.prompt_first, where.prompt_len)
    write_rows(answer_out, out_t[:, answer], rows, where.first, where.answer_len)
    dq_t[...] = jnp.zeros_like(dq_t)

    def run(kv, scores, side, chunks, dkv):
        def step(c, _):
            shares = scores[at(c), :] * inverse[:, side]
            gradients(kv, c, part, shares, side, do_t, both_s, delta[:, side], dkv, dq_t)
            return 0

        lax.fori_loop(0, chunks, step, 0)
        blank(dkv, chunks)

    run(kv, scores, every, chunks, dkv)
    run(answer_kv, answer_scores, answer, where.answer_chunks, answer_dkv)


def own_backward_kernel(
    place, both_s, kv, factors, dq_in, prompt_dq, answer_dq, dkv, dq_t, do_t, q_t
):
    rows = kv.shape[1]
    prompt, answer, every = sides(q_t)
    where = Place(place, rows, kv.shape[0] * rows)
    part = slice(0, rows)
    do_t[...] = both_s[:, VALUES].T
    q_t[...] = both_s[:, KEYS].T
    dq_t[...] = dq_in[...]
    log_total, delta = factors[0:1, :], factors[1:2, :]

    def step(c, _):
        s = masked_scores(kv, c, part, q_t[...], where.own_limit)
        shares = jnp.exp2(s * TO_LOG2 - log_total)
        gradients(kv, c, part, shares, every, do_t, both_s, delta, dkv, dq_t)
        return 0

    lax.fori_loop(0, where.own_chunks, step, 0)
    blank(dkv, where.own_chunks)
    write_rows(prompt_dq, dq_t[:, prompt] * SCALING, rows)
    write_rows(answer_dq, dq_t[:, answer] * SCALING, rows)


def call(kernel, name, arrays, outs, scratch, flops, mib):
    return pl.pallas_call(
        kernel,
        out_shape=[jax.ShapeDtypeStruct(*o) for o in outs],
        in_specs=[SMEM] + [VMEM] * (len(arrays) - 1),
        out_specs=[VMEM] * len(outs),
        scratch_shapes=[pltpu.VMEM(*s) for s in scratch],
        compiler_params=pltpu.CompilerParams(vmem_limit_bytes=mib * 1024 * 1024),
        cost_estimate=pl.CostEstimate(flops=flops, bytes_accessed=0, transcendentals=0),
        name=name,
    )(*arrays)


def copies_of(keys, values, count):
    rows = keys.shape[0]

    def kernel(k, v, out):
        for i in range(count):
            out[i, :, KEYS] = k[...]
            out[i, :, VALUES] = v[...]

    return pl.pallas_call(
        kernel,
        out_shape=jax.ShapeDtypeStruct((count, rows, 2 * HEAD_SIZE), BF16),
        in_specs=[VMEM] * 2,
        out_specs=VMEM,
        compiler_params=pltpu.CompilerParams(vmem_limit_bytes=67043328),
        cost_estimate=pl.CostEstimate(flops=10**6, bytes_accessed=0, transcendentals=0),
        name="copies",
    )(keys, values)


def exchanged(pieces):
    return lax.all_to_all(pieces, "ctx", split_axis=0, concat_axis=0, tiled=True)


def to_partner(block):
    count = lax.axis_size("pair")
    return lax.ppermute(block, "pair", [(i, count - 1 - i) for i in range(count)])


def body(
    prompt_queries,
    prompt_key_rows,
    prompt_value_rows,
    answer_queries,
    response_key_rows,
    response_value_rows,
    prompt_cotangent,
    answer_cotangent,
    prompt_length,
    answer_lengths,
):
    rows = prompt_queries.shape[0]
    lanes = rows * GROUP
    pair_index = lax.axis_index("pair")
    count = lax.axis_size("ctx")
    half = count * rows
    own_kv = exchanged(copies_of(prompt_key_rows, prompt_value_rows, count))
    place = jnp.stack(
        [
            pair_index,
            lax.axis_index("ctx"),
            prompt_length[0],
            lax.dynamic_index_in_dim(answer_lengths, pair_index, keepdims=False),
        ]
    ).astype(jnp.int32)
    wide, tall = (HEAD_SIZE, 2 * lanes), (2 * lanes, 2 * HEAD_SIZE)
    out = ((rows, GROUP * HEAD_SIZE), BF16)
    stat = ((8, 2 * lanes), F32)
    kv_shape = (count, rows, 2 * HEAD_SIZE)
    q_t, both_s, answer_copies = call(
        lambda *refs: prepare_kernel(*refs, half=half),
        "prepare",
        (
            place,
            prompt_queries,
            answer_queries[0],
            prompt_cotangent,
            answer_cotangent[0],
            response_key_rows[0],
            response_value_rows[0],
        ),
        [(wide, BF16), (tall, BF16), (kv_shape, BF16)],
        [],
        10**9,
        8,
    )
    own_kv, answer_copies, q_t, both_s = lax.optimization_barrier(
        (own_kv, answer_copies, q_t, both_s)
    )
    other_kv = to_partner(own_kv)
    answer_kv = exchanged(answer_copies)
    flops = 2 * half * lanes * HEAD_SIZE
    o_t, stats = call(
        own_forward_kernel,
        "own_forward",
        (place, q_t, own_kv),
        [(wide, F32), stat],
        [((half, 2 * lanes), F32)],
        8 * flops,
        16,
    )
    prompt_out, answer_out, other_dkv, answer_dkv, dq_t, factors = call(
        other_kernel,
        "other",
        (place, q_t, both_s, other_kv, answer_kv, o_t, stats),
        [out, out, (kv_shape, BF16), (kv_shape, BF16), (wide, F32), stat],
        [((half, 2 * lanes), F32), ((half, lanes), F32), (wide, F32), (wide, BF16)],
        16 * flops,
        16,
    )
    from_partner = to_partner(other_dkv)
    answer_grad = exchanged(answer_dkv).astype(F32).sum(axis=0).astype(BF16)
    prompt_dq, answer_dq, own_dkv = call(
        own_backward_kernel,
        "own_backward",
        (place, both_s, own_kv, factors, dq_t),
        [out, out, (kv_shape, F32)],
        [(wide, F32), (wide, BF16), (wide, BF16)],
        12 * flops,
        16,
    )
    prompt_dkv = (own_dkv + from_partner.astype(F32)).astype(BF16)
    prompt_grad = exchanged(prompt_dkv).astype(F32).sum(axis=0).astype(BF16)
    return (
        prompt_out,
        answer_out[None],
        prompt_dq,
        prompt_grad[:, KEYS],
        prompt_grad[:, VALUES],
        answer_dq[None],
        answer_grad[None, :, KEYS],
        answer_grad[None, :, VALUES],
    )


def solution(mesh):
    prompt = P(("pair", "ctx"), "head")
    answer = P("pair", "ctx", "head")
    return jax.shard_map(
        body,
        mesh=mesh,
        in_specs=(prompt, prompt, prompt, answer, answer, answer, prompt, answer, P(), P()),
        out_specs=(prompt, answer, prompt, prompt, prompt, answer, answer, answer),
        check_vma=False,
    )
```

```python
import jax
import jax.numpy as jnp
from jax import lax
from jax.experimental import pallas as pl
from jax.experimental.pallas import tpu as pltpu
from jax.sharding import PartitionSpec as P

QUERY_HEADS = 64
KEY_VALUE_HEADS = 8
GROUP = QUERY_HEADS // KEY_VALUE_HEADS
HEAD_SIZE = 128
NEGATIVE = -1e30
SCALING = HEAD_SIZE ** (-0.5)
LOG2E = 1.4426950408889634
TO_LOG2 = SCALING * LOG2E
CHUNK = 512
F32 = jnp.float32
BF16 = jnp.bfloat16
VMEM = pl.BlockSpec(memory_space=pltpu.VMEM)
SMEM = pl.BlockSpec(memory_space=pltpu.SMEM)
KEYS, VALUES = slice(0, HEAD_SIZE), slice(HEAD_SIZE, 2 * HEAD_SIZE)


def dot(a, b, ca, cb):
    return lax.dot_general(a, b, (((ca,), (cb,)), ((), ())), preferred_element_type=F32)


def at(chunk):
    return pl.ds(pl.multiple_of(chunk * CHUNK, CHUNK), CHUNK)


def chunks_of(count):
    return lax.div(count + (CHUNK - 1), CHUNK)


def head(h):
    return slice(h * HEAD_SIZE, (h + 1) * HEAD_SIZE)


class Place:
    def __init__(self, place, rows, half):
        pair, ctx, prompt_len, self.answer_len = (place[i] for i in range(4))
        self.first = ctx * rows
        self.prompt_first = pair * half + self.first
        self.prompt_len = prompt_len
        self.own_len = jnp.clip(prompt_len - pair * half, 1, half)
        self.other_len = jnp.clip(prompt_len - (1 - pair) * half, 1, half)
        self.own_chunks = chunks_of(self.own_len)
        self.other_chunks = chunks_of(self.other_len)
        self.answer_chunks = jnp.where(
            self.first < self.answer_len, chunks_of(self.first + rows), 0
        )
        lane = lax.broadcasted_iota(jnp.int32, (1, rows * GROUP), 1)
        causal = self.first + lax.rem(lane, rows)
        flat = jnp.zeros_like(causal)
        self.own_limit = jnp.concatenate([causal, flat + (self.own_len - 1)], axis=1)
        self.other_limit = jnp.concatenate(
            [flat + jnp.where(pair > 0, half, -1), flat + (self.other_len - 1)], axis=1
        )
        self.answer_limit = causal


def prepare_kernel(
    place,
    prompt_q,
    answer_q,
    prompt_do,
    answer_do,
    answer_k,
    answer_v,
    q_t,
    both_s,
    answer_copies,
    *,
    half,
):
    rows = prompt_q.shape[0]
    for i in range(answer_copies.shape[0]):
        answer_copies[i, :, KEYS] = answer_k[...]
        answer_copies[i, :, VALUES] = answer_v[...]
    lanes = rows * GROUP
    where = Place(place, rows, half)
    for k, (q_ref, do_ref, first, length) in enumerate(
        (
            (prompt_q, prompt_do, where.prompt_first, where.prompt_len),
            (answer_q, answer_do, where.first, where.answer_len),
        )
    ):
        live = first + lax.broadcasted_iota(jnp.int32, (rows, HEAD_SIZE), 0) < length
        q_rows = jnp.concatenate([q_ref[:, head(h)] for h in range(GROUP)], axis=0)
        do_rows = jnp.concatenate(
            [
                jnp.where(live, do_ref[:, head(h)].astype(F32), 0.0).astype(BF16)
                for h in range(GROUP)
            ],
            axis=0,
        )
        side = slice(k * lanes, (k + 1) * lanes)
        both_s[side, KEYS] = q_rows
        both_s[side, VALUES] = do_rows
        q_t[:, side] = q_rows.T


def block_of(kv, c, part, cols):
    rows = part.stop - part.start
    count = CHUNK // rows
    return kv[pl.ds(c * count, count), part, cols].reshape(CHUNK, HEAD_SIZE)


def put_block(dkv, c, dk, dv):
    rows = dkv.shape[1]
    count = CHUNK // rows
    for cols, d in ((KEYS, dk), (VALUES, dv)):
        dkv[pl.ds(c * count, count), :, cols] = d.astype(dkv.dtype).reshape(count, rows, HEAD_SIZE)


def masked_scores(kv, c, part, q_t, limit):
    s = dot(block_of(kv, c, part, KEYS), q_t, 1, 0)
    key = lax.broadcasted_iota(jnp.int32, s.shape, 0)
    return jnp.where(key <= limit - c * CHUNK, s, NEGATIVE)


def score_pass(kv, part, q_t, side, limit, chunks, scores):
    def step(c, run):
        s = masked_scores(kv, c, part, q_t[:, side], limit)
        scores[at(c), :] = s
        for k in range(CHUNK // 8):
            run = jnp.maximum(run, s[k * 8 : (k + 1) * 8])
        return run

    start = jnp.full((8, side.stop - side.start), NEGATIVE, F32)
    return lax.fori_loop(0, chunks, step, start)


def value_pass(kv, part, side, row_max, chunks, scores, o_t):
    def step(c, sums):
        p = jnp.exp2(scores[at(c), :] * TO_LOG2 - row_max)
        for k in range(CHUNK // 8):
            sums = sums + p[k * 8 : (k + 1) * 8]
        scores[at(c), :] = p
        o_t[:, side] += dot(block_of(kv, c, part, VALUES), p.astype(BF16), 0, 0)
        return sums

    start = jnp.zeros((8, side.stop - side.start), F32)
    return jnp.sum(lax.fori_loop(0, chunks, step, start), axis=0, keepdims=True)


def gradients(kv, c, part, shares, side, do_t, both_s, delta, dkv, dq_t):
    dp = dot(block_of(kv, c, part, VALUES), do_t[:, side], 1, 0)
    ds = (shares * (dp - delta)).astype(BF16)
    put_block(
        dkv,
        c,
        dot(ds, both_s[side, KEYS], 1, 0) * SCALING,
        dot(shares.astype(BF16), both_s[side, VALUES], 1, 0),
    )
    dq_t[:, side] += dot(block_of(kv, c, part, KEYS), ds, 0, 0)


def blank(dkv, begin):
    def step(c, _):
        zero = jnp.zeros((CHUNK, HEAD_SIZE), F32)
        put_block(dkv, c, zero, zero)
        return 0

    lax.fori_loop(begin, dkv.shape[0] * dkv.shape[1] // CHUNK, step, 0)


def write_rows(ref, block_t, rows, first=None, length=None):
    block = block_t.T
    for h in range(GROUP):
        piece = block[h * rows : (h + 1) * rows]
        if first is not None:
            live = first + lax.broadcasted_iota(jnp.int32, (rows, HEAD_SIZE), 0) < length
            piece = jnp.where(live, piece, 0.0)
        ref[:, head(h)] = piece.astype(BF16)


def sides(q_t):
    lanes = q_t.shape[1] // 2
    return slice(0, lanes), slice(lanes, 2 * lanes), slice(0, 2 * lanes)


def own_forward_kernel(place, q_t, kv, o_t, stats, scores):
    rows = kv.shape[1]
    every = sides(q_t)[2]
    where = Place(place, rows, kv.shape[0] * rows)
    part = slice(0, rows)
    run = score_pass(kv, part, q_t, every, where.own_limit, where.own_chunks, scores)
    row_max = jnp.max(run, axis=0, keepdims=True) * TO_LOG2
    o_t[...] = jnp.zeros_like(o_t)
    stats[0:1, :] = row_max
    stats[1:2, :] = value_pass(kv, part, every, row_max, where.own_chunks, scores, o_t)


def other_kernel(
    place,
    q_t,
    both_s,
    kv,
    answer_kv,
    o_in,
    stats,
    prompt_out,
    answer_out,
    dkv,
    answer_dkv,
    dq_t,
    factors,
    scores,
    answer_scores,
    o_t,
    do_t,
):
    rows = kv.shape[1]
    prompt, answer, every = sides(q_t)
    where = Place(place, rows, kv.shape[0] * rows)
    part = slice(0, rows)
    chunks = where.other_chunks
    run = score_pass(kv, part, q_t, every, where.other_limit, chunks, scores)
    answer_run = score_pass(
        answer_kv, part, q_t, answer, where.answer_limit, where.answer_chunks, answer_scores
    )
    run = jnp.concatenate([run[:, prompt], jnp.maximum(run[:, answer], answer_run)], axis=1)
    do_t[...] = both_s[:, VALUES].T
    own_max = stats[0:1, :]
    row_max = jnp.maximum(jnp.max(run, axis=0, keepdims=True) * TO_LOG2, own_max)
    shrink = jnp.exp2(own_max - row_max)
    o_t[...] = o_in[...] * shrink
    total = value_pass(kv, part, every, row_max, chunks, scores, o_t) + stats[1:2, :] * shrink
    answer_total = value_pass(
        answer_kv, part, answer, row_max[:, answer], where.answer_chunks, answer_scores, o_t
    )
    total = jnp.concatenate([total[:, prompt], total[:, answer] + answer_total], axis=1)
    inverse = 1.0 / total
    out_t = o_t[...] * inverse
    delta = jnp.sum(do_t[...].astype(F32) * out_t, axis=0, keepdims=True)
    factors[0:1, :] = row_max + jnp.log(total) * LOG2E
    factors[1:2, :] = delta
    write_rows(prompt_out, out_t[:, prompt], rows, where.prompt_first, where.prompt_len)
    write_rows(answer_out, out_t[:, answer], rows, where.first, where.answer_len)
    dq_t[...] = jnp.zeros_like(dq_t)

    def run(kv, scores, side, chunks, dkv):
        def step(c, _):
            shares = scores[at(c), :] * inverse[:, side]
            gradients(kv, c, part, shares, side, do_t, both_s, delta[:, side], dkv, dq_t)
            return 0

        lax.fori_loop(0, chunks, step, 0)
        blank(dkv, chunks)

    run(kv, scores, every, chunks, dkv)
    run(answer_kv, answer_scores, answer, where.answer_chunks, answer_dkv)


def own_backward_kernel(
    place, both_s, kv, factors, dq_in, prompt_dq, answer_dq, dkv, dq_t, do_t, q_t
):
    rows = kv.shape[1]
    prompt, answer, every = sides(q_t)
    where = Place(place, rows, kv.shape[0] * rows)
    part = slice(0, rows)
    do_t[...] = both_s[:, VALUES].T
    q_t[...] = both_s[:, KEYS].T
    dq_t[...] = dq_in[...]
    log_total, delta = factors[0:1, :], factors[1:2, :]

    def step(c, _):
        s = masked_scores(kv, c, part, q_t[...], where.own_limit)
        shares = jnp.exp2(s * TO_LOG2 - log_total)
        gradients(kv, c, part, shares, every, do_t, both_s, delta, dkv, dq_t)
        return 0

    lax.fori_loop(0, where.own_chunks, step, 0)
    blank(dkv, where.own_chunks)
    write_rows(prompt_dq, dq_t[:, prompt] * SCALING, rows)
    write_rows(answer_dq, dq_t[:, answer] * SCALING, rows)


def call(kernel, name, arrays, outs, scratch, flops, mib):
    return pl.pallas_call(
        kernel,
        out_shape=[jax.ShapeDtypeStruct(*o) for o in outs],
        in_specs=[SMEM] + [VMEM] * (len(arrays) - 1),
        out_specs=[VMEM] * len(outs),
        scratch_shapes=[pltpu.VMEM(*s) for s in scratch],
        compiler_params=pltpu.CompilerParams(vmem_limit_bytes=mib * 1024 * 1024),
        cost_estimate=pl.CostEstimate(flops=flops, bytes_accessed=0, transcendentals=0),
        name=name,
    )(*arrays)


def copies_of(keys, values, count):
    rows = keys.shape[0]

    def kernel(k, v, out):
        for i in range(count):
            out[i, :, KEYS] = k[...]
            out[i, :, VALUES] = v[...]

    return pl.pallas_call(
        kernel,
        out_shape=jax.ShapeDtypeStruct((count, rows, 2 * HEAD_SIZE), BF16),
        in_specs=[VMEM] * 2,
        out_specs=VMEM,
        compiler_params=pltpu.CompilerParams(vmem_limit_bytes=67043328),
        cost_estimate=pl.CostEstimate(flops=10**6, bytes_accessed=0, transcendentals=0),
        name="copies",
    )(keys, values)


def exchanged(pieces):
    return lax.all_to_all(pieces, "ctx", split_axis=0, concat_axis=0, tiled=True)


def to_partner(block):
    count = lax.axis_size("pair")
    return lax.ppermute(block, "pair", [(i, count - 1 - i) for i in range(count)])


def body(
    prompt_queries,
    prompt_key_rows,
    prompt_value_rows,
    answer_queries,
    response_key_rows,
    response_value_rows,
    prompt_cotangent,
    answer_cotangent,
    prompt_length,
    answer_lengths,
):
    rows = prompt_queries.shape[0]
    lanes = rows * GROUP
    pair_index = lax.axis_index("pair")
    count = lax.axis_size("ctx")
    half = count * rows
    own_kv = exchanged(copies_of(prompt_key_rows, prompt_value_rows, count))
    place = jnp.stack(
        [
            pair_index,
            lax.axis_index("ctx"),
            prompt_length[0],
            lax.dynamic_index_in_dim(answer_lengths, pair_index, keepdims=False),
        ]
    ).astype(jnp.int32)
    wide, tall = (HEAD_SIZE, 2 * lanes), (2 * lanes, 2 * HEAD_SIZE)
    out = ((rows, GROUP * HEAD_SIZE), BF16)
    stat = ((8, 2 * lanes), F32)
    kv_shape = (count, rows, 2 * HEAD_SIZE)
    q_t, both_s, answer_copies = call(
        lambda *refs: prepare_kernel(*refs, half=half),
        "prepare",
        (
            place,
            prompt_queries,
            answer_queries[0],
            prompt_cotangent,
            answer_cotangent[0],
            response_key_rows[0],
            response_value_rows[0],
        ),
        [(wide, BF16), (tall, BF16), (kv_shape, BF16)],
        [],
        10**9,
        8,
    )
    own_kv, answer_copies, q_t, both_s = lax.optimization_barrier(
        (own_kv, answer_copies, q_t, both_s)
    )
    other_kv = to_partner(own_kv)
    answer_kv = exchanged(answer_copies)
    flops = 2 * half * lanes * HEAD_SIZE
    o_t, stats = call(
        own_forward_kernel,
        "own_forward",
        (place, q_t, own_kv),
        [(wide, F32), stat],
        [((half, 2 * lanes), F32)],
        8 * flops,
        16,
    )
    prompt_out, answer_out, other_dkv, answer_dkv, dq_t, factors = call(
        other_kernel,
        "other",
        (place, q_t, both_s, other_kv, answer_kv, o_t, stats),
        [out, out, (kv_shape, BF16), (kv_shape, BF16), (wide, F32), stat],
        [((half, 2 * lanes), F32), ((half, lanes), F32), (wide, F32), (wide, BF16)],
        16 * flops,
        16,
    )
    from_partner = to_partner(other_dkv)
    answer_grad = exchanged(answer_dkv).astype(F32).sum(axis=0).astype(BF16)
    prompt_dq, answer_dq, own_dkv = call(
        own_backward_kernel,
        "own_backward",
        (place, both_s, own_kv, factors, dq_t),
        [out, out, (kv_shape, F32)],
        [(wide, F32), (wide, BF16), (wide, BF16)],
        12 * flops,
        16,
    )
    prompt_dkv = (own_dkv + from_partner.astype(F32)).astype(BF16)
    prompt_grad = exchanged(prompt_dkv).astype(F32).sum(axis=0).astype(BF16)
    return (
        prompt_out,
        answer_out[None],
        prompt_dq,
        prompt_grad[:, KEYS],
        prompt_grad[:, VALUES],
        answer_dq[None],
        answer_grad[None, :, KEYS],
        answer_grad[None, :, VALUES],
    )


def solution(mesh):
    prompt = P(("pair", "ctx"), "head")
    answer = P("pair", "ctx", "head")
    return jax.shard_map(
        body,
        mesh=mesh,
        in_specs=(prompt, prompt, prompt, answer, answer, answer, prompt, answer, P(), P()),
        out_specs=(prompt, answer, prompt, prompt, prompt, answer, answer, answer),
        check_vma=False,
    )
```

```python
import jax
import jax.numpy as jnp
from jax import lax
from jax.experimental import pallas as pl
from jax.experimental.pallas import tpu as pltpu
from jax.sharding import PartitionSpec as P

QUERY_HEADS = 64
KEY_VALUE_HEADS = 8
GROUP = QUERY_HEADS // KEY_VALUE_HEADS
HEAD_SIZE = 128
NEGATIVE = -1e30
SCALING = HEAD_SIZE ** (-0.5)
LOG2E = 1.4426950408889634
TO_LOG2 = SCALING * LOG2E
CHUNK = 512
F32 = jnp.float32
BF16 = jnp.bfloat16
VMEM = pl.BlockSpec(memory_space=pltpu.VMEM)
SMEM = pl.BlockSpec(memory_space=pltpu.SMEM)
KEYS, VALUES = slice(0, HEAD_SIZE), slice(HEAD_SIZE, 2 * HEAD_SIZE)


def dot(a, b, ca, cb):
    return lax.dot_general(a, b, (((ca,), (cb,)), ((), ())), preferred_element_type=F32)


def at(chunk, size):
    return pl.ds(pl.multiple_of(chunk * size, size), size)


def chunks_of(count):
    return lax.div(count + (CHUNK - 1), CHUNK)


def head(h):
    return slice(h * HEAD_SIZE, (h + 1) * HEAD_SIZE)


class Place:
    def __init__(self, place, rows, half):
        pair, ctx, prompt_len, self.answer_len = (place[i] for i in range(4))
        self.first = ctx * rows
        self.prompt_first = pair * half + self.first
        self.prompt_len = prompt_len
        self.own_len = jnp.clip(prompt_len - pair * half, 1, half)
        self.other_len = jnp.clip(prompt_len - (1 - pair) * half, 1, half)
        self.own_chunks = chunks_of(self.own_len)
        lane = lax.broadcasted_iota(jnp.int32, (1, rows * GROUP), 1)
        causal = self.first + lax.rem(lane, rows)
        flat = jnp.zeros_like(causal)
        self.own_limit = jnp.concatenate([causal, flat + (self.own_len - 1)], axis=1)
        self.other_limit = jnp.concatenate(
            [flat + jnp.where(pair > 0, half, -1), flat + (self.other_len - 1)], axis=1
        )
        self.answer_limit = causal


def prepare_kernel(
    place,
    prompt_q,
    answer_q,
    prompt_do,
    answer_do,
    q_t,
    both_s,
    *,
    half,
):
    rows = prompt_q.shape[0]
    lanes = rows * GROUP
    where = Place(place, rows, half)
    for k, (q_ref, do_ref, first, length) in enumerate(
        (
            (prompt_q, prompt_do, where.prompt_first, where.prompt_len),
            (answer_q, answer_do, where.first, where.answer_len),
        )
    ):
        live = first + lax.broadcasted_iota(jnp.int32, (rows, HEAD_SIZE), 0) < length
        q_rows = jnp.concatenate([q_ref[:, head(h)] for h in range(GROUP)], axis=0)
        do_rows = jnp.concatenate(
            [
                jnp.where(live, do_ref[:, head(h)].astype(F32), 0.0).astype(BF16)
                for h in range(GROUP)
            ],
            axis=0,
        )
        side = slice(k * lanes, (k + 1) * lanes)
        both_s[side, KEYS] = q_rows
        both_s[side, VALUES] = do_rows
        q_t[:, side] = q_rows.T


def block_of(kv, c, cols, size):
    count = size // kv.shape[1]
    return kv[at(c, count), :, cols].reshape(size, HEAD_SIZE)


def put_block(dkv, c, dk, dv):
    size, rows = dk.shape[0], dkv.shape[1]
    count = size // rows
    for cols, d in ((KEYS, dk), (VALUES, dv)):
        dkv[at(c, count), :, cols] = d.astype(dkv.dtype).reshape(count, rows, HEAD_SIZE)


def masked_scores(kv, c, q_t, limit, size):
    s = dot(block_of(kv, c, KEYS, size), q_t, 1, 0)
    key = lax.broadcasted_iota(jnp.int32, s.shape, 0)
    return jnp.where(key <= limit - c * size, s, NEGATIVE)


def score_pass(kv, q_t, side, limit, chunks, size, scores):
    def step(c, run):
        s = masked_scores(kv, c, q_t[:, side], limit, size)
        scores[at(c, size), :] = s
        for k in range(size // 8):
            run = jnp.maximum(run, s[k * 8 : (k + 1) * 8])
        return run

    return lax.fori_loop(0, chunks, step, jnp.full((8, side.stop - side.start), NEGATIVE, F32))


def value_pass(kv, side, row_max, chunks, size, scores, o_t):
    def step(c, sums):
        p = jnp.exp2(scores[at(c, size), :] * TO_LOG2 - row_max)
        for k in range(size // 8):
            sums = sums + p[k * 8 : (k + 1) * 8]
        scores[at(c, size), :] = p
        o_t[:, side] += dot(block_of(kv, c, VALUES, size), p.astype(BF16), 0, 0)
        return sums

    sums = lax.fori_loop(0, chunks, step, jnp.zeros((8, side.stop - side.start), F32))
    return jnp.sum(sums, axis=0, keepdims=True)


def gradients(kv, c, size, shares, side, do_t, both_s, delta, dkv, dq_t):
    dp = dot(block_of(kv, c, VALUES, size), do_t[:, side], 1, 0)
    ds = (shares * (dp - delta)).astype(BF16)
    put_block(
        dkv,
        c,
        dot(ds, both_s[side, KEYS], 1, 0) * SCALING,
        dot(shares.astype(BF16), both_s[side, VALUES], 1, 0),
    )
    dq_t[:, side] += dot(block_of(kv, c, KEYS, size), ds, 0, 0)


def blank(dkv, begin):
    def step(c, _):
        zero = jnp.zeros((CHUNK, HEAD_SIZE), F32)
        put_block(dkv, c, zero, zero)
        return 0

    lax.fori_loop(begin, dkv.shape[0] * dkv.shape[1] // CHUNK, step, 0)


def write_rows(ref, block_t, rows, first=None, length=None):
    block = block_t.T
    for h in range(GROUP):
        piece = block[h * rows : (h + 1) * rows]
        if first is not None:
            live = first + lax.broadcasted_iota(jnp.int32, (rows, HEAD_SIZE), 0) < length
            piece = jnp.where(live, piece, 0.0)
        ref[:, head(h)] = piece.astype(BF16)


def sides(q_t):
    lanes = q_t.shape[1] // 2
    return slice(0, lanes), slice(lanes, 2 * lanes), slice(0, 2 * lanes)


def own_forward_kernel(place, q_t, kv, o_t, stats, scores):
    rows = kv.shape[1]
    every = sides(q_t)[2]
    where = Place(place, rows, kv.shape[0] * rows)
    run = score_pass(kv, q_t, every, where.own_limit, where.own_chunks, CHUNK, scores)
    row_max = jnp.max(run, axis=0, keepdims=True) * TO_LOG2
    o_t[...] = jnp.zeros_like(o_t)
    stats[0:1, :] = row_max
    stats[1:2, :] = value_pass(kv, every, row_max, where.own_chunks, CHUNK, scores, o_t)


def other_kernel(
    place,
    q_t,
    both_s,
    kv,
    answer_kv,
    o_in,
    stats,
    prompt_out,
    answer_out,
    dkv,
    answer_dkv,
    dq_t,
    factors,
    scores,
    answer_scores,
    o_t,
    do_t,
):
    rows = kv.shape[1]
    prompt, answer, every = sides(q_t)
    where = Place(place, rows, kv.shape[0] * rows)
    size = kv.shape[0] * rows
    pieces = jnp.minimum(where.prompt_len, 1)
    run = score_pass(kv, q_t, every, where.other_limit, pieces, size, scores)
    answer_run = score_pass(answer_kv, q_t, answer, where.answer_limit, pieces, size, answer_scores)
    run = jnp.concatenate([run[:, prompt], jnp.maximum(run[:, answer], answer_run)], axis=1)
    do_t[...] = both_s[:, VALUES].T
    own_max = stats[0:1, :]
    row_max = jnp.maximum(jnp.max(run, axis=0, keepdims=True) * TO_LOG2, own_max)
    shrink = jnp.exp2(own_max - row_max)
    o_t[...] = o_in[...] * shrink
    total = value_pass(kv, every, row_max, pieces, size, scores, o_t) + stats[1:2, :] * shrink
    answer_total = value_pass(
        answer_kv, answer, row_max[:, answer], pieces, size, answer_scores, o_t
    )
    total = jnp.concatenate([total[:, prompt], total[:, answer] + answer_total], axis=1)
    inverse = 1.0 / total
    out_t = o_t[...] * inverse
    delta = jnp.sum(do_t[...].astype(F32) * out_t, axis=0, keepdims=True)
    factors[0:1, :] = row_max + jnp.log(total) * LOG2E
    factors[1:2, :] = delta
    write_rows(prompt_out, out_t[:, prompt], rows, where.prompt_first, where.prompt_len)
    write_rows(answer_out, out_t[:, answer], rows, where.first, where.answer_len)
    dq_t[...] = jnp.zeros_like(dq_t)

    for kv, scores, side, dkv in (
        (kv, scores, every, dkv),
        (answer_kv, answer_scores, answer, answer_dkv),
    ):

        def step(c, _, kv=kv, scores=scores, side=side, dkv=dkv):
            shares = scores[at(c, size), :] * inverse[:, side]
            gradients(kv, c, size, shares, side, do_t, both_s, delta[:, side], dkv, dq_t)
            return 0

        lax.fori_loop(0, pieces, step, 0)


def own_backward_kernel(
    place, both_s, kv, factors, dq_in, prompt_dq, answer_dq, dkv, dq_t, do_t, q_t
):
    rows = kv.shape[1]
    prompt, answer, every = sides(q_t)
    where = Place(place, rows, kv.shape[0] * rows)
    do_t[...] = both_s[:, VALUES].T
    q_t[...] = both_s[:, KEYS].T
    dq_t[...] = dq_in[...]
    log_total, delta = factors[0:1, :], factors[1:2, :]

    def step(c, _):
        s = masked_scores(kv, c, q_t[...], where.own_limit, CHUNK)
        shares = jnp.exp2(s * TO_LOG2 - log_total)
        gradients(kv, c, CHUNK, shares, every, do_t, both_s, delta, dkv, dq_t)
        return 0

    lax.fori_loop(0, where.own_chunks, step, 0)
    blank(dkv, where.own_chunks)
    write_rows(prompt_dq, dq_t[:, prompt] * SCALING, rows)
    write_rows(answer_dq, dq_t[:, answer] * SCALING, rows)


def call(kernel, name, arrays, outs, scratch, flops, mib):
    return pl.pallas_call(
        kernel,
        out_shape=[jax.ShapeDtypeStruct(*o) for o in outs],
        in_specs=[SMEM] + [VMEM] * (len(arrays) - 1),
        out_specs=[VMEM] * len(outs),
        scratch_shapes=[pltpu.VMEM(*s) for s in scratch],
        compiler_params=pltpu.CompilerParams(vmem_limit_bytes=mib * 1024 * 1024),
        cost_estimate=pl.CostEstimate(flops=flops, bytes_accessed=0, transcendentals=0),
        name=name,
    )(*arrays)


def copies_of(parts, count):
    shape = jax.ShapeDtypeStruct((count, parts[0].shape[0], 2 * HEAD_SIZE), BF16)

    def kernel(pk, pv, ak, av, prompt, answer):
        for k, v, out in ((pk, pv, prompt), (ak, av, answer)):
            for i in range(count):
                out[i, :, KEYS] = k[...]
                out[i, :, VALUES] = v[...]

    return pl.pallas_call(
        kernel,
        out_shape=[shape] * 2,
        in_specs=[VMEM] * 4,
        out_specs=[VMEM] * 2,
        compiler_params=pltpu.CompilerParams(vmem_limit_bytes=67043328),
        cost_estimate=pl.CostEstimate(flops=10**6, bytes_accessed=0, transcendentals=0),
        name="copies",
    )(*parts)


def collected(prompt_parts, answer_parts):
    shape = jax.ShapeDtypeStruct((prompt_parts.shape[1], HEAD_SIZE), BF16)

    def kernel(prompt_parts, answer_parts, prompt_k, prompt_v, answer_k, answer_v):
        for parts, k, v in (
            (prompt_parts, prompt_k, prompt_v),
            (answer_parts, answer_k, answer_v),
        ):
            total = jnp.sum(parts[...].astype(F32), axis=0).astype(BF16)
            k[...] = total[:, KEYS]
            v[...] = total[:, VALUES]

    return pl.pallas_call(
        kernel,
        out_shape=[shape] * 4,
        in_specs=[VMEM] * 2,
        out_specs=[VMEM] * 4,
        compiler_params=pltpu.CompilerParams(vmem_limit_bytes=16 * 1024 * 1024),
        name="collected",
    )(prompt_parts, answer_parts)


def exchanged(pieces):
    return lax.all_to_all(pieces, "ctx", split_axis=0, concat_axis=0, tiled=True)


def to_partner(block):
    count = lax.axis_size("pair")
    return lax.ppermute(block, "pair", [(i, count - 1 - i) for i in range(count)])


def body(
    prompt_queries,
    prompt_key_rows,
    prompt_value_rows,
    answer_queries,
    response_key_rows,
    response_value_rows,
    prompt_cotangent,
    answer_cotangent,
    prompt_length,
    answer_lengths,
):
    rows = prompt_queries.shape[0]
    lanes = rows * GROUP
    pair_index = lax.axis_index("pair")
    count = lax.axis_size("ctx")
    half = count * rows
    prompt_copies, answer_copies = copies_of(
        (prompt_key_rows, prompt_value_rows, response_key_rows[0], response_value_rows[0]), count
    )
    own_kv, answer_copies, prompt_length, answer_lengths = lax.optimization_barrier(
        (exchanged(prompt_copies), answer_copies, prompt_length, answer_lengths)
    )
    other_kv = to_partner(own_kv)
    answer_kv = exchanged(answer_copies)
    place = jnp.stack(
        [
            pair_index,
            lax.axis_index("ctx"),
            prompt_length[0],
            lax.dynamic_index_in_dim(answer_lengths, pair_index, keepdims=False),
        ]
    ).astype(jnp.int32)
    wide, tall = (HEAD_SIZE, 2 * lanes), (2 * lanes, 2 * HEAD_SIZE)
    out = ((rows, GROUP * HEAD_SIZE), BF16)
    stat = ((8, 2 * lanes), F32)
    kv_shape = (count, rows, 2 * HEAD_SIZE)
    q_t, both_s = call(
        lambda *refs: prepare_kernel(*refs, half=half),
        "prepare",
        (place, prompt_queries, answer_queries[0], prompt_cotangent, answer_cotangent[0]),
        [(wide, BF16), (tall, BF16)],
        [],
        10**9,
        8,
    )
    flops = 2 * half * lanes * HEAD_SIZE
    o_t, stats = call(
        own_forward_kernel,
        "own_forward",
        (place, q_t, own_kv),
        [(wide, F32), stat],
        [((half, 2 * lanes), F32)],
        8 * flops,
        16,
    )
    prompt_out, answer_out, other_dkv, answer_dkv, dq_t, factors = call(
        other_kernel,
        "other",
        (place, q_t, both_s, other_kv, answer_kv, o_t, stats),
        [out, out, (kv_shape, BF16), (kv_shape, BF16), (wide, F32), stat],
        [((half, 2 * lanes), F32), ((half, lanes), F32), (wide, F32), (wide, BF16)],
        16 * flops,
        16,
    )
    from_partner = to_partner(other_dkv)
    answer_parts = exchanged(answer_dkv)
    prompt_dq, answer_dq, own_dkv = call(
        own_backward_kernel,
        "own_backward",
        (place, both_s, own_kv, factors, dq_t),
        [out, out, (kv_shape, F32)],
        [(wide, F32), (wide, BF16), (wide, BF16)],
        12 * flops,
        16,
    )
    prompt_dkv = (own_dkv + from_partner.astype(F32)).astype(BF16)
    prompt_parts = exchanged(prompt_dkv)
    prompt_k, prompt_v, answer_k, answer_v = collected(prompt_parts, answer_parts)
    return (
        prompt_out,
        answer_out[None],
        prompt_dq,
        prompt_k,
        prompt_v,
        answer_dq[None],
        answer_k[None],
        answer_v[None],
    )


def solution(mesh):
    prompt = P(("pair", "ctx"), "head")
    answer = P("pair", "ctx", "head")
    return jax.shard_map(
        body,
        mesh=mesh,
        in_specs=(prompt, prompt, prompt, answer, answer, answer, prompt, answer, P(), P()),
        out_specs=(prompt, answer, prompt, prompt, prompt, answer, answer, answer),
        check_vma=False,
    )
```

```python
import jax
import jax.numpy as jnp
from jax import lax
from jax.experimental import pallas as pl
from jax.experimental.pallas import tpu as pltpu
from jax.sharding import PartitionSpec as P

QUERY_HEADS = 64
KEY_VALUE_HEADS = 8
GROUP = QUERY_HEADS // KEY_VALUE_HEADS
HEAD_SIZE = 128
NEGATIVE = -1e30
SCALING = HEAD_SIZE ** (-0.5)
LOG2E = 1.4426950408889634
TO_LOG2 = SCALING * LOG2E
CHUNK = 512
F32 = jnp.float32
BF16 = jnp.bfloat16
VMEM = pl.BlockSpec(memory_space=pltpu.VMEM)
SMEM = pl.BlockSpec(memory_space=pltpu.SMEM)
KEYS, VALUES = slice(0, HEAD_SIZE), slice(HEAD_SIZE, 2 * HEAD_SIZE)


def dot(a, b, ca, cb):
    return lax.dot_general(a, b, (((ca,), (cb,)), ((), ())), preferred_element_type=F32)


def at(chunk, size):
    return pl.ds(pl.multiple_of(chunk * size, size), size)


def chunks_of(count):
    return lax.div(count + (CHUNK - 1), CHUNK)


def head(h):
    return slice(h * HEAD_SIZE, (h + 1) * HEAD_SIZE)


class Place:
    def __init__(self, place, rows, half):
        pair, ctx, prompt_len, self.answer_len = (place[i] for i in range(4))
        self.first = ctx * rows
        self.prompt_first = pair * half + self.first
        self.prompt_len = prompt_len
        self.own_len = jnp.clip(prompt_len - pair * half, 1, half)
        self.other_len = jnp.clip(prompt_len - (1 - pair) * half, 1, half)
        self.own_chunks = chunks_of(self.own_len)
        lane = lax.broadcasted_iota(jnp.int32, (1, rows * GROUP), 1)
        causal = self.first + lax.rem(lane, rows)
        flat = jnp.zeros_like(causal)
        self.own_limit = jnp.concatenate([causal, flat + (self.own_len - 1)], axis=1)
        self.other_limit = jnp.concatenate(
            [flat + jnp.where(pair > 0, half, -1), flat + (self.other_len - 1)], axis=1
        )
        self.answer_limit = causal


def prepare_kernel(
    place,
    prompt_q,
    answer_q,
    prompt_do,
    answer_do,
    answer_k,
    answer_v,
    q_t,
    both_s,
    answer_copies,
    *,
    half,
):
    rows = prompt_q.shape[0]
    for i in range(answer_copies.shape[0]):
        answer_copies[i, :, KEYS] = answer_k[...]
        answer_copies[i, :, VALUES] = answer_v[...]
    lanes = rows * GROUP
    where = Place(place, rows, half)
    for k, (q_ref, do_ref, first, length) in enumerate(
        (
            (prompt_q, prompt_do, where.prompt_first, where.prompt_len),
            (answer_q, answer_do, where.first, where.answer_len),
        )
    ):
        live = first + lax.broadcasted_iota(jnp.int32, (rows, HEAD_SIZE), 0) < length
        q_rows = jnp.concatenate([q_ref[:, head(h)] for h in range(GROUP)], axis=0)
        do_rows = jnp.concatenate(
            [
                jnp.where(live, do_ref[:, head(h)].astype(F32), 0.0).astype(BF16)
                for h in range(GROUP)
            ],
            axis=0,
        )
        side = slice(k * lanes, (k + 1) * lanes)
        both_s[side, KEYS] = q_rows
        both_s[side, VALUES] = do_rows
        q_t[:, side] = q_rows.T


def block_of(kv, c, cols, size):
    count = size // kv.shape[1]
    return kv[at(c, count), :, cols].reshape(size, HEAD_SIZE)


def put_block(dkv, c, dk, dv):
    size, rows = dk.shape[0], dkv.shape[1]
    count = size // rows
    for cols, d in ((KEYS, dk), (VALUES, dv)):
        dkv[at(c, count), :, cols] = d.astype(dkv.dtype).reshape(count, rows, HEAD_SIZE)


def masked_scores(kv, c, q_t, limit, size):
    s = dot(block_of(kv, c, KEYS, size), q_t, 1, 0)
    key = lax.broadcasted_iota(jnp.int32, s.shape, 0)
    return jnp.where(key <= limit - c * size, s, NEGATIVE)


def score_pass(kv, q_t, side, limit, chunks, size, scores):
    def step(c, run):
        s = masked_scores(kv, c, q_t[:, side], limit, size)
        scores[at(c, size), :] = s
        for k in range(size // 8):
            run = jnp.maximum(run, s[k * 8 : (k + 1) * 8])
        return run

    return lax.fori_loop(0, chunks, step, jnp.full((8, side.stop - side.start), NEGATIVE, F32))


def value_pass(kv, side, row_max, chunks, size, scores, o_t):
    def step(c, sums):
        p = jnp.exp2(scores[at(c, size), :] * TO_LOG2 - row_max)
        for k in range(size // 8):
            sums = sums + p[k * 8 : (k + 1) * 8]
        scores[at(c, size), :] = p
        o_t[:, side] += dot(block_of(kv, c, VALUES, size), p.astype(BF16), 0, 0)
        return sums

    sums = lax.fori_loop(0, chunks, step, jnp.zeros((8, side.stop - side.start), F32))
    return jnp.sum(sums, axis=0, keepdims=True)


def gradients(kv, c, size, shares, side, do_t, both_s, delta, dkv, dq_t):
    dp = dot(block_of(kv, c, VALUES, size), do_t[:, side], 1, 0)
    ds = (shares * (dp - delta)).astype(BF16)
    put_block(
        dkv,
        c,
        dot(ds, both_s[side, KEYS], 1, 0) * SCALING,
        dot(shares.astype(BF16), both_s[side, VALUES], 1, 0),
    )
    dq_t[:, side] += dot(block_of(kv, c, KEYS, size), ds, 0, 0)


def blank(dkv, begin):
    def step(c, _):
        zero = jnp.zeros((CHUNK, HEAD_SIZE), F32)
        put_block(dkv, c, zero, zero)
        return 0

    lax.fori_loop(begin, dkv.shape[0] * dkv.shape[1] // CHUNK, step, 0)


def write_rows(ref, block_t, rows, first=None, length=None):
    block = block_t.T
    for h in range(GROUP):
        piece = block[h * rows : (h + 1) * rows]
        if first is not None:
            live = first + lax.broadcasted_iota(jnp.int32, (rows, HEAD_SIZE), 0) < length
            piece = jnp.where(live, piece, 0.0)
        ref[:, head(h)] = piece.astype(BF16)


def sides(q_t):
    lanes = q_t.shape[1] // 2
    return slice(0, lanes), slice(lanes, 2 * lanes), slice(0, 2 * lanes)


def own_forward_kernel(place, q_t, kv, o_t, stats, scores):
    rows = kv.shape[1]
    every = sides(q_t)[2]
    where = Place(place, rows, kv.shape[0] * rows)
    run = score_pass(kv, q_t, every, where.own_limit, where.own_chunks, CHUNK, scores)
    row_max = jnp.max(run, axis=0, keepdims=True) * TO_LOG2
    o_t[...] = jnp.zeros_like(o_t)
    stats[0:1, :] = row_max
    stats[1:2, :] = value_pass(kv, every, row_max, where.own_chunks, CHUNK, scores, o_t)


def other_kernel(
    place,
    q_t,
    both_s,
    kv,
    answer_kv,
    o_in,
    stats,
    prompt_out,
    answer_out,
    dkv,
    answer_dkv,
    dq_t,
    factors,
    scores,
    answer_scores,
    o_t,
    do_t,
):
    rows = kv.shape[1]
    prompt, answer, every = sides(q_t)
    where = Place(place, rows, kv.shape[0] * rows)
    size = kv.shape[0] * rows
    pieces = jnp.minimum(where.prompt_len, 1)
    run = score_pass(kv, q_t, every, where.other_limit, pieces, size, scores)
    answer_run = score_pass(answer_kv, q_t, answer, where.answer_limit, pieces, size, answer_scores)
    run = jnp.concatenate([run[:, prompt], jnp.maximum(run[:, answer], answer_run)], axis=1)
    do_t[...] = both_s[:, VALUES].T
    own_max = stats[0:1, :]
    row_max = jnp.maximum(jnp.max(run, axis=0, keepdims=True) * TO_LOG2, own_max)
    shrink = jnp.exp2(own_max - row_max)
    o_t[...] = o_in[...] * shrink
    total = value_pass(kv, every, row_max, pieces, size, scores, o_t) + stats[1:2, :] * shrink
    answer_total = value_pass(
        answer_kv, answer, row_max[:, answer], pieces, size, answer_scores, o_t
    )
    total = jnp.concatenate([total[:, prompt], total[:, answer] + answer_total], axis=1)
    inverse = 1.0 / total
    out_t = o_t[...] * inverse
    delta = jnp.sum(do_t[...].astype(F32) * out_t, axis=0, keepdims=True)
    factors[0:1, :] = row_max + jnp.log(total) * LOG2E
    factors[1:2, :] = delta
    write_rows(prompt_out, out_t[:, prompt], rows, where.prompt_first, where.prompt_len)
    write_rows(answer_out, out_t[:, answer], rows, where.first, where.answer_len)
    dq_t[...] = jnp.zeros_like(dq_t)

    for kv, scores, side, dkv in (
        (kv, scores, every, dkv),
        (answer_kv, answer_scores, answer, answer_dkv),
    ):

        def step(c, _, kv=kv, scores=scores, side=side, dkv=dkv):
            shares = scores[at(c, size), :] * inverse[:, side]
            gradients(kv, c, size, shares, side, do_t, both_s, delta[:, side], dkv, dq_t)
            return 0

        lax.fori_loop(0, pieces, step, 0)


def own_backward_kernel(
    place, both_s, kv, factors, dq_in, prompt_dq, answer_dq, dkv, dq_t, do_t, q_t
):
    rows = kv.shape[1]
    prompt, answer, every = sides(q_t)
    where = Place(place, rows, kv.shape[0] * rows)
    do_t[...] = both_s[:, VALUES].T
    q_t[...] = both_s[:, KEYS].T
    dq_t[...] = dq_in[...]
    log_total, delta = factors[0:1, :], factors[1:2, :]

    def step(c, _):
        s = masked_scores(kv, c, q_t[...], where.own_limit, CHUNK)
        shares = jnp.exp2(s * TO_LOG2 - log_total)
        gradients(kv, c, CHUNK, shares, every, do_t, both_s, delta, dkv, dq_t)
        return 0

    lax.fori_loop(0, where.own_chunks, step, 0)
    blank(dkv, where.own_chunks)
    write_rows(prompt_dq, dq_t[:, prompt] * SCALING, rows)
    write_rows(answer_dq, dq_t[:, answer] * SCALING, rows)


def call(kernel, name, arrays, outs, scratch, flops, mib, aliases=None):
    return pl.pallas_call(
        kernel,
        out_shape=[jax.ShapeDtypeStruct(*o) for o in outs],
        in_specs=[SMEM] + [VMEM] * (len(arrays) - 1),
        out_specs=[VMEM] * len(outs),
        scratch_shapes=[pltpu.VMEM(*s) for s in scratch],
        input_output_aliases=aliases or {},
        compiler_params=pltpu.CompilerParams(vmem_limit_bytes=mib * 1024 * 1024),
        cost_estimate=pl.CostEstimate(flops=flops, bytes_accessed=0, transcendentals=0),
        name=name,
    )(*arrays)


def copies_of(keys, values, count):
    rows = keys.shape[0]

    def kernel(k, v, out):
        for i in range(count):
            out[i, :, KEYS] = k[...]
            out[i, :, VALUES] = v[...]

    return pl.pallas_call(
        kernel,
        out_shape=jax.ShapeDtypeStruct((count, rows, 2 * HEAD_SIZE), BF16),
        in_specs=[VMEM] * 2,
        out_specs=VMEM,
        compiler_params=pltpu.CompilerParams(vmem_limit_bytes=67043328),
        cost_estimate=pl.CostEstimate(flops=10**6, bytes_accessed=0, transcendentals=0),
        name="copies",
    )(keys, values)


def collected(prompt_parts, answer_parts):
    shape = jax.ShapeDtypeStruct((prompt_parts.shape[1], HEAD_SIZE), BF16)

    def kernel(prompt_parts, answer_parts, prompt_k, prompt_v, answer_k, answer_v):
        for parts, k, v in (
            (prompt_parts, prompt_k, prompt_v),
            (answer_parts, answer_k, answer_v),
        ):
            total = jnp.sum(parts[...].astype(F32), axis=0).astype(BF16)
            k[...] = total[:, KEYS]
            v[...] = total[:, VALUES]

    return pl.pallas_call(
        kernel,
        out_shape=[shape] * 4,
        in_specs=[VMEM] * 2,
        out_specs=[VMEM] * 4,
        compiler_params=pltpu.CompilerParams(vmem_limit_bytes=16 * 1024 * 1024),
        name="collected",
    )(prompt_parts, answer_parts)


def exchanged(pieces):
    return lax.all_to_all(pieces, "ctx", split_axis=0, concat_axis=0, tiled=True)


def to_partner(block):
    count = lax.axis_size("pair")
    return lax.ppermute(block, "pair", [(i, count - 1 - i) for i in range(count)])


def body(
    prompt_queries,
    prompt_key_rows,
    prompt_value_rows,
    answer_queries,
    response_key_rows,
    response_value_rows,
    prompt_cotangent,
    answer_cotangent,
    prompt_length,
    answer_lengths,
):
    rows = prompt_queries.shape[0]
    lanes = rows * GROUP
    pair_index = lax.axis_index("pair")
    count = lax.axis_size("ctx")
    half = count * rows
    own_kv = exchanged(copies_of(prompt_key_rows, prompt_value_rows, count))
    place = jnp.stack(
        [
            pair_index,
            lax.axis_index("ctx"),
            prompt_length[0],
            lax.dynamic_index_in_dim(answer_lengths, pair_index, keepdims=False),
        ]
    ).astype(jnp.int32)
    wide, tall = (HEAD_SIZE, 2 * lanes), (2 * lanes, 2 * HEAD_SIZE)
    out = ((rows, GROUP * HEAD_SIZE), BF16)
    stat = ((8, 2 * lanes), F32)
    kv_shape = (count, rows, 2 * HEAD_SIZE)
    q_t, both_s, answer_copies = call(
        lambda *refs: prepare_kernel(*refs, half=half),
        "prepare",
        (
            place,
            prompt_queries,
            answer_queries[0],
            prompt_cotangent,
            answer_cotangent[0],
            response_key_rows[0],
            response_value_rows[0],
        ),
        [(wide, BF16), (tall, BF16), (kv_shape, BF16)],
        [],
        10**9,
        8,
    )
    own_kv, answer_copies, q_t, both_s = lax.optimization_barrier(
        (own_kv, answer_copies, q_t, both_s)
    )
    other_kv = to_partner(own_kv)
    answer_kv = exchanged(answer_copies)
    flops = 2 * half * lanes * HEAD_SIZE
    o_t, stats = call(
        own_forward_kernel,
        "own_forward",
        (place, q_t, own_kv),
        [(wide, F32), stat],
        [((half, 2 * lanes), F32)],
        8 * flops,
        16,
    )
    prompt_out, answer_out, other_dkv, answer_dkv, dq_t, factors = call(
        other_kernel,
        "other",
        (place, q_t, both_s, other_kv, answer_kv, o_t, stats),
        [out, out, (kv_shape, BF16), (kv_shape, BF16), (wide, F32), stat],
        [((half, 2 * lanes), F32), ((half, lanes), F32), (wide, F32), (wide, BF16)],
        16 * flops,
        16,
        aliases={5: 4},
    )
    from_partner = to_partner(other_dkv)
    answer_parts = exchanged(answer_dkv)
    prompt_dq, answer_dq, own_dkv = call(
        own_backward_kernel,
        "own_backward",
        (place, both_s, own_kv, factors, dq_t),
        [out, out, (kv_shape, F32)],
        [(wide, F32), (wide, BF16), (wide, BF16)],
        12 * flops,
        16,
    )
    prompt_dkv = (own_dkv + from_partner.astype(F32)).astype(BF16)
    prompt_parts = exchanged(prompt_dkv)
    prompt_k, prompt_v, answer_k, answer_v = collected(prompt_parts, answer_parts)
    return (
        prompt_out,
        answer_out[None],
        prompt_dq,
        prompt_k,
        prompt_v,
        answer_dq[None],
        answer_k[None],
        answer_v[None],
    )


def solution(mesh):
    prompt = P(("pair", "ctx"), "head")
    answer = P("pair", "ctx", "head")
    return jax.shard_map(
        body,
        mesh=mesh,
        in_specs=(prompt, prompt, prompt, answer, answer, answer, prompt, answer, P(), P()),
        out_specs=(prompt, answer, prompt, prompt, prompt, answer, answer, answer),
        check_vma=False,
    )
```
